32 devices in a mesh: groups: 2 (over y), ell: 4 (over z), batch: 4 (over x, core).
Axes of the slice: x: 2, y: 2, z: 4, core: 2. Of those that a mesh axis runs over, the one named last changes fastest.
Arguments:
- hidden_act: bfloat16 [128, 1024], P('groups'), parts along dimension 0, may hold values from -1.5 to 1.5
- weight: bfloat16 [8, 1024, 8192], P('groups', 'batch', 'ell'), parts along dimension 0, may hold values from -0.09375 to 0.09375
- first_moment: float32 [8, 1024, 8192], P('groups', 'batch', 'ell'), parts along dimension 0, may hold values from -3 to 3
- second_moment: float32 [8, 1024, 8192], P('groups', 'batch', 'ell'), parts along dimension 0, may hold values from 0.05 to 1
- wigner: bfloat16 [4, 8192, 8192], P(None, 'ell', 'batch'), may hold values from -0.0625 to 0.0625
- quad_weight: float32 [8192], P('batch'), may hold values from 0.5 to 2
- target: bfloat16 [6, 64, 8192], P('groups', None, 'ell'), parts along dimension 0, may hold values from -9 to 9
Outputs:
- new_weight: bfloat16 [8, 1024, 8192], P('groups', 'batch', 'ell'), parts along dimension 0
- new_first: float32 [8, 1024, 8192], P('groups', 'batch', 'ell'), parts along dimension 0
- new_second: float32 [8, 1024, 8192], P('groups', 'batch', 'ell'), parts along dimension 0
The draws below stay inside these ranges and needn't reach their ends.
There are 2 independent parts, one for each index of `groups`. The reference program is written for one: setup_inputs(seed, part) draws one part's arguments, and reference() takes and returns one part's arrays. A program takes and returns all parts, laid end to end along the dimension named above; an argument that names none is the same for every part. Nothing has to cross between parts.
All inputs are finite; a program needn't handle non-finite values.
Results may differ from the reference program's by a relative error of at most 0.012.
Values may be sent and summed in bfloat16 or wider, within the bound.
No kernel may reach another device: no remote copies, remote signals or barrier semaphores. Data moves between devices by JAX's collectives and lax.ppermute only.
A program may use at most 128 MiB of HBM per device.

```python
import math
import jax
import jax.numpy as jnp
from jax import lax

H = 1024
L = 8192
A = 8192
B = 64
N_ELL = 4
N_BATCH = 4


def draw_hidden_act(key, part):
    value_key = jax.random.fold_in(key, 11)
    result = jnp.clip(0.5 * jax.random.normal(value_key, (B, H), jnp.float32), -1.5, 1.5)
    return result.astype(jnp.bfloat16)


def shard_levels(own_key, extent, shards, least, top_value):
    level = 1.0
    for position, blocks in shards:
        steps = jax.random.uniform(jax.random.fold_in(jax.random.fold_in(own_key, 6), position), (blocks,), jnp.float32, least / len(shards), top_value / len(shards))
        level = level * jnp.repeat(jnp.exp(steps), extent[position] // blocks).reshape((-1,) + (1,) * (len(extent) - 1 - position))
    return level


def noise(key, shape, deviation, limit, cuts=(), held_as=jnp.bfloat16):
    loudness = shard_levels(key, shape, cuts, -0.22, 0.18) if cuts else 1.0
    values = jax.random.normal(key, shape, jnp.float32) * deviation * loudness
    return jnp.minimum(jnp.maximum(values, -limit), limit).astype(held_as)


def setup_inputs(seed: int = 0, part: int = 0) -> dict:
    streams_of = jax.random.split(jax.random.key(seed), 8)
    part_keys = jax.random.split(jax.random.fold_in(streams_of[7], part), 8)
    hidden_act = draw_hidden_act(jax.random.fold_in(jax.random.fold_in(streams_of[7], part), 71), part)
    weight = noise(part_keys[1], (4, H, L), (4 * H) ** -0.5, 0.09375, ((1, 4), (2, 4)))
    first_moment = noise(part_keys[2], (4, H, L), 0.5, 3.0, ((1, 4), (2, 4)), jnp.float32)
    second_moment = jnp.clip(jnp.exp(math.log(1.0) - 2.9957323 * jax.random.uniform(part_keys[3], (4, H, L), jnp.float32) ** shard_levels(part_keys[3], (4, H, L), ((1, 4), (2, 4)), -0.2, 0.2)), 0.05, 1.0)
    wigner = noise(streams_of[4], (4, L, A), L ** -0.5, 0.0625, ((1, 4), (2, 4)))
    quad_weight = jnp.clip(jnp.exp(math.log(2.0) - 1.3862944 * jax.random.uniform(streams_of[5], (A,), jnp.float32) ** shard_levels(streams_of[5], (A,), ((0, 4),), -0.2, 0.2)), 0.5, 2.0)
    target = noise(part_keys[6], (3, B, L), 1.5, 9.0, ((2, 4),))
    return dict(hidden_act=hidden_act, weight=weight, first_moment=first_moment, second_moment=second_moment, wigner=wigner, quad_weight=quad_weight, target=target)


row_table = (0, 0, 1, 1, 2, 2, 3)
highest = lax.Precision.HIGHEST
first_fix = 0.9999734386
second_fix = 0.0952078528

def rounded(value):
    return lax.optimization_barrier(value.astype(jnp.bfloat16)).astype(jnp.float32)

def block_sum(count, term, shape):

    def step(index, total):
        return total + rounded(term(index))
    return lax.fori_loop(0, count, step, jnp.zeros(shape, jnp.float32))

def reference(hidden_act, weight, first_moment, second_moment, wigner, quad_weight, target):
    hidden_f = hidden_act.astype(jnp.float32)
    log_power = jnp.einsum('cj,sjl->scl', hidden_f, weight.astype(jnp.float32), precision=highest)
    multipole = jnp.arange(L, dtype=jnp.int32).astype(jnp.float32)
    lens_rate = multipole * (multipole + 1.0) / (float(L) * float(L))
    loss_weight = 1.0 + 2.0 * multipole / float(L)
    power_temp = jnp.exp(log_power[0])
    power_pol = jnp.exp(log_power[2])
    cross_scale = jnp.exp(0.5 * (log_power[0] + log_power[2]))
    cross_ratio = jnp.tanh(log_power[1])
    power_cross = cross_ratio * cross_scale
    power_lens = jnp.exp(log_power[3])
    rows = rounded(jnp.stack([power_temp, lens_rate * power_temp, power_cross, lens_rate * power_cross, power_pol, lens_rate * power_pol, power_lens]))
    order = jnp.array(row_table, dtype=jnp.int32)
    l_block = L // N_ELL
    a_block = A // N_BATCH

    def forward_block(index):
        start = (index * l_block).astype(jnp.int32)
        part_rows = lax.dynamic_slice_in_dim(rows, start, l_block, 2)
        part_tab = lax.dynamic_slice_in_dim(wigner, start, l_block, 1)[order].astype(jnp.float32)
        return jnp.einsum('rcl,rla->rca', part_rows, part_tab, precision=highest)
    angle_sums = block_sum(N_ELL, forward_block, (7, B, A))
    lensed_corr = angle_sums[0:6:2] - angle_sums[6:7] * angle_sums[1:6:2]
    back_rows = rounded(lensed_corr * quad_weight)

    def back_block(index):
        start = (index * a_block).astype(jnp.int32)
        part = lax.dynamic_slice_in_dim(back_rows, start, a_block, 2)
        part_tab = lax.dynamic_slice_in_dim(wigner[0:3], start, a_block, 2).astype(jnp.float32)
        return jnp.einsum('xca,xla->xcl', part, part_tab, precision=highest)
    lensed_power = block_sum(N_BATCH, back_block, (3, B, L))
    residual_grad = rounded(loss_weight * (lensed_power - target.astype(jnp.float32)) / B)

    def grad_block(index):
        start = (index * l_block).astype(jnp.int32)
        part = lax.dynamic_slice_in_dim(residual_grad, start, l_block, 2)
        part_tab = lax.dynamic_slice_in_dim(wigner[0:3], start, l_block, 1).astype(jnp.float32)
        return jnp.einsum('xcl,xla->xca', part, part_tab, precision=highest)
    corr_grad = block_sum(N_ELL, grad_block, (3, B, A)) * quad_weight
    lens_sigma = angle_sums[6:7]
    sigma_grad = -lax.optimization_barrier(jnp.sum(corr_grad * angle_sums[1:6:2], axis=0, keepdims=True))
    term_grad = rounded(jnp.concatenate([corr_grad[0:1], -lens_sigma * corr_grad[0:1], corr_grad[1:2], -lens_sigma * corr_grad[1:2], corr_grad[2:3], -lens_sigma * corr_grad[2:3], sigma_grad], 0))

    def row_block(index):
        start = (index * a_block).astype(jnp.int32)
        part = lax.dynamic_slice_in_dim(term_grad, start, a_block, 2)
        part_tab = lax.dynamic_slice_in_dim(wigner, start, a_block, 2)[order].astype(jnp.float32)
        return jnp.einsum('rca,rla->rcl', part, part_tab, precision=highest)
    row_grad = block_sum(N_BATCH, row_block, (7, B, L))
    temp_coef = row_grad[0] + lens_rate * row_grad[1]
    cross_coef = row_grad[2] + lens_rate * row_grad[3]
    pol_coef = row_grad[4] + lens_rate * row_grad[5]
    log_grad = rounded(jnp.stack([temp_coef * power_temp + 0.5 * cross_coef * power_cross, cross_coef * (1.0 - cross_ratio * cross_ratio) * cross_scale, pol_coef * power_pol + 0.5 * cross_coef * power_cross, row_grad[6] * power_lens]))
    weight_grad = jnp.einsum('cj,scl->sjl', hidden_f, log_grad, precision=highest)
    new_first = 0.9 * first_moment + 0.1 * weight_grad
    new_second = 0.999 * second_moment + 0.001 * weight_grad * weight_grad
    update = new_first / first_fix / (jnp.sqrt(new_second / second_fix) + 1e-08)
    new_weight = (weight.astype(jnp.float32) - 0.001 * update).astype(jnp.bfloat16)
    return (new_weight, new_first, new_second)
```

```python
import jax
import jax.numpy as jnp
from jax import lax
from jax.experimental import pallas as pl
from jax.experimental.pallas import tpu as pltpu
from jax.sharding import PartitionSpec as P

L = 8192


first_fix = 0.9999734386
second_fix = 0.0952078528


def forward_terms(rows, wigner):
    parts = []
    for table in range(3):
        parts.append(
            jnp.einsum(
                "rcl,la->rca",
                rows[2 * table : 2 * table + 2],
                wigner[table],
                preferred_element_type=jnp.float32,
            )
        )
    parts.append(
        jnp.einsum("rcl,la->rca", rows[6:7], wigner[3], preferred_element_type=jnp.float32)
    )
    return jnp.concatenate(parts, 0)


def backward_terms(piece, tables):
    parts = []
    for table in range(3):
        parts.append(
            jnp.einsum(
                "rca,la->rcl",
                piece[2 * table : 2 * table + 2],
                tables[table],
                preferred_element_type=jnp.float32,
            )
        )
    parts.append(
        jnp.einsum("rca,la->rcl", piece[6:7], tables[3], preferred_element_type=jnp.float32)
    )
    return jnp.concatenate(parts, 0)


def angle_reduce(partial_value):
    return lax.psum(partial_value.astype(jnp.bfloat16), "ell").astype(jnp.float32)


def angle_apply(share, work, init):
    return work(init, share, 0)


def multipole_reduce(partial_value):
    return lax.psum(partial_value.astype(jnp.bfloat16), "batch").astype(jnp.float32)


def local_plain(hidden_act, weight, first_moment, second_moment, wigner, quad_weight, target):
    batch_rows = hidden_act.shape[0]
    h_local = weight.shape[1]
    l_local = weight.shape[2]
    ell_start = lax.axis_index("ell") * l_local
    multipole = (ell_start + lax.iota(jnp.int32, l_local)).astype(jnp.float32)
    lens_rate = multipole * (multipole + 1.0) / (float(L) * float(L))
    loss_weight = 1.0 + 2.0 * multipole / float(L)
    own_hidden = lax.dynamic_slice_in_dim(hidden_act, lax.axis_index("batch") * h_local, h_local, 1)
    local_terms = jnp.einsum("cj,sjl->scl", own_hidden, weight, preferred_element_type=jnp.float32)
    log_power = lax.psum(local_terms, "batch")
    power_temp = jnp.exp(log_power[0])
    power_pol = jnp.exp(log_power[2])
    cross_scale = jnp.exp(0.5 * (log_power[0] + log_power[2]))
    cross_ratio = jnp.tanh(log_power[1])
    power_cross = cross_ratio * cross_scale
    power_lens = jnp.exp(log_power[3])
    rows = jnp.stack(
        [
            power_temp,
            lens_rate * power_temp,
            power_cross,
            lens_rate * power_cross,
            power_pol,
            lens_rate * power_pol,
            power_lens,
        ]
    ).astype(jnp.bfloat16)
    angle_sums = angle_reduce(forward_terms(rows, wigner))
    lensed_corr = angle_sums[0:6:2] - angle_sums[6:7] * angle_sums[1:6:2]
    back_rows = (lensed_corr * quad_weight).astype(jnp.bfloat16)

    def project_back(total, piece, start):
        return jnp.stack(
            [
                jnp.einsum(
                    "ca,la->cl", piece[table], wigner[table], preferred_element_type=jnp.float32
                )
                for table in range(3)
            ]
        )

    back_empty = jnp.zeros((3, batch_rows, l_local), jnp.float32)
    lensed_power = multipole_reduce(angle_apply(back_rows, project_back, back_empty))
    residual_grad = (loss_weight * (lensed_power - target.astype(jnp.float32)) / batch_rows).astype(
        jnp.bfloat16
    )
    back_partial = jnp.stack(
        [
            jnp.einsum(
                "cl,la->ca", residual_grad[table], wigner[table], preferred_element_type=jnp.float32
            )
            for table in range(3)
        ]
    )
    corr_grad = angle_reduce(back_partial) * quad_weight
    lens_sigma = angle_sums[6:7]
    sigma_grad = -jnp.sum(corr_grad * angle_sums[1:6:2], axis=0, keepdims=True)
    term_grad = jnp.concatenate(
        [
            corr_grad[0:1],
            -lens_sigma * corr_grad[0:1],
            corr_grad[1:2],
            -lens_sigma * corr_grad[1:2],
            corr_grad[2:3],
            -lens_sigma * corr_grad[2:3],
            sigma_grad,
        ],
        0,
    ).astype(jnp.bfloat16)

    def project_rows(total, piece, start):
        return backward_terms(piece, wigner)

    row_empty = jnp.zeros((7, batch_rows, l_local), jnp.float32)
    row_grad = multipole_reduce(angle_apply(term_grad, project_rows, row_empty))
    temp_coef = row_grad[0] + lens_rate * row_grad[1]
    cross_coef = row_grad[2] + lens_rate * row_grad[3]
    pol_coef = row_grad[4] + lens_rate * row_grad[5]
    log_grad = jnp.stack(
        [
            temp_coef * power_temp + 0.5 * cross_coef * power_cross,
            cross_coef * (1.0 - cross_ratio * cross_ratio) * cross_scale,
            pol_coef * power_pol + 0.5 * cross_coef * power_cross,
            row_grad[6] * power_lens,
        ]
    ).astype(jnp.bfloat16)
    weight_grad = jnp.einsum(
        "cj,scl->sjl", own_hidden, log_grad, preferred_element_type=jnp.float32
    )
    new_first = 0.9 * first_moment + 0.1 * weight_grad
    new_second = 0.999 * second_moment + 0.001 * weight_grad * weight_grad
    update = new_first / first_fix / (jnp.sqrt(new_second / second_fix) + 1e-08)
    new_weight = (weight.astype(jnp.float32) - 0.001 * update).astype(jnp.bfloat16)
    return (new_weight, new_first, new_second)


bf16 = jnp.bfloat16
f32 = jnp.float32
ORDER = (0, 2, 1, 3)


def swap(value, axis, mask):
    count = lax.axis_size(axis)
    return lax.ppermute(value, axis, [(i, i ^ mask) for i in range(count)])


def scatter(keep, send, axis):
    half = keep.shape[0] // 2
    near = keep + swap(send, axis, 1).astype(f32)
    return near[:half] + swap(near[half:].astype(bf16), axis, 2).astype(f32)


def gather(own, axis):
    far = swap(own, axis, 2)
    near = swap(own, axis, 1)
    return (own, near, far, swap(far, axis, 1))


def call(kernel, out_shape, *args, in_hbm=(), scratch=(), aliases=None, flops=0, moved=0):
    vmem = pl.BlockSpec(memory_space=pltpu.VMEM)
    hbm = pl.BlockSpec(memory_space=pl.ANY)
    return pl.pallas_call(
        kernel,
        out_shape=out_shape,
        in_specs=[hbm if i in in_hbm else vmem for i in range(len(args))],
        out_specs=jax.tree.map(lambda _: vmem, out_shape),
        scratch_shapes=list(scratch),
        compiler_params=pltpu.CompilerParams(vmem_limit_bytes=8 << 20),
        cost_estimate=pl.CostEstimate(flops=flops, transcendentals=0, bytes_accessed=moved),
    )(*args)


def fetch_table(wigner, table):
    _, rows, cols = wigner.shape
    pieces = 8
    step = rows // pieces

    def kernel(source, out, sem):
        copies = [
            pltpu.make_async_copy(
                source.at[table, pl.ds(i * step, step)], out.at[pl.ds(i * step, step)], sem.at[i]
            )
            for i in range(pieces)
        ]
        for copy in copies:
            copy.start()
        for copy in copies:
            copy.wait()

    return call(
        kernel,
        pltpu.VMEM((rows, cols), bf16),
        wigner,
        in_hbm=(0,),
        scratch=[pltpu.SemaphoreType.DMA((pieces,))],
        moved=rows * cols * 4,
    )


def fill(lhs, chunks, second):
    rows = chunks[0].shape[0]
    for place, position in enumerate(ORDER):
        value = chunks[position][...]
        if second is None:
            lhs[place * rows : (place + 1) * rows] = value
        else:
            lhs[2 * place * rows : (2 * place + 1) * rows] = value
            lhs[(2 * place + 1) * rows : (2 * place + 2) * rows] = second(position, value)


def onto_angles(chunks, table, rate=None):
    kinds = 1 if rate is None else 2
    rows = 4 * kinds * chunks[0].shape[0]
    depth, cols = table.shape
    step = cols // 4

    def kernel(*refs):
        parts, rest = refs[:4], refs[4:]
        if rate is None:
            tab, keep, send, lhs = rest
            second = None
        else:
            rate_ref, tab, keep, send, lhs = rest

            def second(_, value):
                return (value.astype(f32) * rate_ref[...]).astype(bf16)

        fill(lhs, parts, second)
        for i in range(4):
            cut = slice(i * step, (i + 1) * step)
            total = jnp.dot(lhs[...], tab[:, cut], preferred_element_type=f32)
            keep[:, cut] = total[: rows // 2]
            send[:, cut] = total[rows // 2 :].astype(bf16)

    args = list(chunks) + ([] if rate is None else [rate]) + [table]
    return call(
        kernel,
        (
            jax.ShapeDtypeStruct((rows // 2, cols), f32),
            jax.ShapeDtypeStruct((rows // 2, cols), bf16),
        ),
        *args,
        scratch=[pltpu.VMEM((rows, depth), bf16)],
        flops=2 * rows * depth * cols,
        moved=rows * cols * 6,
    )


def onto_multipoles(chunks, table, sigma=None, rate=None):
    kinds = 1 if rate is None else 2
    count = chunks[0].shape[0]
    rows = 4 * kinds * count
    cols, depth = table.shape
    step = cols // 4

    def kernel(*refs):
        parts, rest = refs[:4], refs[4:]
        if rate is None:
            tab, keep, send, lhs = rest
            second = None
        else:
            sigmas, (rate_ref, tab, keep, send, lhs) = rest[:4], rest[4:]

            def second(position, value):
                return (-(value.astype(f32) * sigmas[position][...].astype(f32))).astype(bf16)

        fill(lhs, parts, second)
        for i in range(4):
            cut = slice(i * step, (i + 1) * step)
            total = lax.dot_general(
                tab[cut, :], lhs[...], (((1,), (1,)), ((), ())), preferred_element_type=f32
            ).T
            for place in range(4):
                if rate is None:
                    value = total[place * count : (place + 1) * count]
                else:
                    value = (
                        total[2 * place * count : (2 * place + 1) * count]
                        + total[(2 * place + 1) * count : (2 * place + 2) * count]
                        * rate_ref[:, cut]
                    )
                if place < 2:
                    keep[place * count : (place + 1) * count, cut] = value
                else:
                    send[(place - 2) * count : (place - 1) * count, cut] = value.astype(bf16)

    args = list(chunks) + ([] if rate is None else list(sigma) + [rate]) + [table]
    return call(
        kernel,
        (
            jax.ShapeDtypeStruct((2 * count, cols), f32),
            jax.ShapeDtypeStruct((2 * count, cols), bf16),
        ),
        *args,
        scratch=[pltpu.VMEM((rows, depth), bf16)],
        flops=2 * rows * depth * cols,
        moved=count * cols * 12,
    )


def spectra(hidden, weight):
    rows, depth = hidden.shape
    kinds, _, cols = weight.shape

    def kernel(hid, wgt, keep, send):
        total = jnp.dot(hid[...], wgt[...], preferred_element_type=f32)
        keep[...] = total[: rows // 2]
        send[...] = total[rows // 2 :].astype(bf16)

    out = pl.BlockSpec((None, rows // 2, cols), lambda s: (s, 0, 0))
    return pl.pallas_call(
        kernel,
        grid=(kinds,),
        out_shape=(
            jax.ShapeDtypeStruct((kinds, rows // 2, cols), f32),
            jax.ShapeDtypeStruct((kinds, rows // 2, cols), bf16),
        ),
        in_specs=[
            pl.BlockSpec((rows, depth), lambda s: (0, 0)),
            pl.BlockSpec((None, depth, cols), lambda s: (s, 0, 0)),
        ],
        out_specs=(out, out),
        compiler_params=pltpu.CompilerParams(vmem_limit_bytes=12 << 20),
    )(hidden, weight)


def adam(hidden, log_grad, weight, first, second):
    rows, depth = hidden.shape
    kinds, _, cols = weight.shape
    tile = depth // 2

    def kernel(hid, grad, wgt, one, two, new_wgt, new_one, new_two):
        slope = lax.dot_general(
            hid[...], grad[...], (((0,), (0,)), ((), ())), preferred_element_type=f32
        )
        moved = 0.9 * one[...] + 0.1 * slope
        spread = 0.999 * two[...] + 0.001 * slope * slope
        new_one[...] = moved
        new_two[...] = spread
        update = moved * (1.0 / first_fix) / (jnp.sqrt(spread * (1.0 / second_fix)) + 1e-08)
        new_wgt[...] = (wgt[...].astype(f32) - 0.001 * update).astype(bf16)

    block = pl.BlockSpec((None, tile, cols), lambda s, i: (s, i, 0))
    return pl.pallas_call(
        kernel,
        grid=(kinds, depth // tile),
        out_shape=(
            jax.ShapeDtypeStruct(weight.shape, bf16),
            jax.ShapeDtypeStruct(weight.shape, f32),
            jax.ShapeDtypeStruct(weight.shape, f32),
        ),
        in_specs=[
            pl.BlockSpec((rows, tile), lambda s, i: (0, i)),
            pl.BlockSpec((None, rows, cols), lambda s, i: (s, 0, 0)),
            block,
            block,
            block,
        ],
        out_specs=(block, block, block),
        compiler_params=pltpu.CompilerParams(vmem_limit_bytes=24 << 20),
    )(hidden, log_grad, weight, first, second)


def local_fast(hidden_act, weight, first_moment, second_moment, wigner, quad_weight, target):
    count = hidden_act.shape[0] // 4
    h_local = weight.shape[1]
    l_local = weight.shape[2]
    at_ell = lax.axis_index("ell")
    at_batch = lax.axis_index("batch")
    chunk = jnp.bitwise_xor(at_ell, at_batch)
    multipole = (at_ell * l_local + lax.iota(jnp.int32, l_local)).astype(f32)[None]
    lens_rate = multipole * (multipole + 1.0) / (float(L) * float(L))
    loss_weight = (1.0 + 2.0 * multipole / float(L)) / hidden_act.shape[0]
    quad = quad_weight[None]
    own_hidden = jnp.concatenate(
        [
            lax.dynamic_slice(
                hidden_act,
                (jnp.bitwise_xor(chunk, position) * count, at_batch * h_local),
                (count, h_local),
            )
            for position in ORDER
        ]
    )
    own_target = lax.dynamic_slice_in_dim(target, chunk * count, count, 1).astype(f32)

    keep, send = spectra(own_hidden, weight)
    table = {t: fetch_table(wigner, t) for t in (3, 0, 2, 1)}
    log_power = {s: scatter(keep[s], send[s], "batch") for s in (3, 0, 2, 1)}
    power_lens = jnp.exp(log_power[3])
    power_temp = jnp.exp(log_power[0])
    power_pol = jnp.exp(log_power[2])
    cross_scale = jnp.exp(0.5 * (log_power[0] + log_power[2]))
    cross_ratio = jnp.tanh(log_power[1])
    power_cross = cross_ratio * cross_scale

    def sums_of(power, t, rate):
        return scatter(*onto_angles(gather(power.astype(bf16), "batch"), table[t], rate), "ell")

    sigma = sums_of(power_lens, 3, None)
    all_sigma = gather(sigma.astype(bf16), "ell")
    corr_grad = {}
    second_sum = {}
    for x, power in ((0, power_temp), (2, power_pol), (1, power_cross)):
        sums = sums_of(power, x, lens_rate)
        first_sum, second_sum[x] = sums[:count], sums[count:]
        back_row = ((first_sum - sigma * second_sum[x]) * quad).astype(bf16)
        lensed = scatter(*onto_multipoles(gather(back_row, "ell"), table[x]), "batch")
        residual = (loss_weight * (lensed - own_target[x])).astype(bf16)
        corr_grad[x] = scatter(*onto_angles(gather(residual, "batch"), table[x]), "ell") * quad

    coef = {}
    for x in (0, 2, 1):
        coef[x] = scatter(
            *onto_multipoles(
                gather(corr_grad[x].astype(bf16), "ell"), table[x], all_sigma, lens_rate
            ),
            "batch",
        )
    sigma_grad = -sum(corr_grad[x] * second_sum[x] for x in range(3))
    coef[3] = scatter(
        *onto_multipoles(gather(sigma_grad.astype(bf16), "ell"), table[3]), "batch"
    )
    half_cross = 0.5 * coef[1] * power_cross
    log_grad = (
        coef[0] * power_temp + half_cross,
        coef[1] * (1.0 - cross_ratio * cross_ratio) * cross_scale,
        coef[2] * power_pol + half_cross,
        coef[3] * power_lens,
    )
    log_grad = [gather(value.astype(bf16), "batch") for value in log_grad]
    log_grad = jnp.stack(
        [jnp.concatenate([value[position] for position in ORDER]) for value in log_grad]
    )
    return adam(own_hidden, log_grad, weight, first_moment, second_moment)


def solution(mesh):
    four = mesh.shape["ell"] == 4 and mesh.shape["batch"] == 4
    return jax.shard_map(
        local_fast if four else local_plain,
        mesh=mesh,
        in_specs=(
            P("groups", None),
            P("groups", "batch", "ell"),
            P("groups", "batch", "ell"),
            P("groups", "batch", "ell"),
            P(None, "ell", "batch"),
            P("batch"),
            P("groups", None, "ell"),
        ),
        out_specs=(
            P("groups", "batch", "ell"),
            P("groups", "batch", "ell"),
            P("groups", "batch", "ell"),
        ),
        check_vma=False,
    )
```

```python
import jax
import jax.numpy as jnp
from jax import lax
from jax.experimental import pallas as pl
from jax.experimental.pallas import tpu as pltpu
from jax.sharding import PartitionSpec as P

L = 8192


first_fix = 0.9999734386
second_fix = 0.0952078528


def forward_terms(rows, wigner):
    parts = []
    for table in range(3):
        parts.append(
            jnp.einsum(
                "rcl,la->rca",
                rows[2 * table : 2 * table + 2],
                wigner[table],
                preferred_element_type=jnp.float32,
            )
        )
    parts.append(
        jnp.einsum("rcl,la->rca", rows[6:7], wigner[3], preferred_element_type=jnp.float32)
    )
    return jnp.concatenate(parts, 0)


def backward_terms(piece, tables):
    parts = []
    for table in range(3):
        parts.append(
            jnp.einsum(
                "rca,la->rcl",
                piece[2 * table : 2 * table + 2],
                tables[table],
                preferred_element_type=jnp.float32,
            )
        )
    parts.append(
        jnp.einsum("rca,la->rcl", piece[6:7], tables[3], preferred_element_type=jnp.float32)
    )
    return jnp.concatenate(parts, 0)


def angle_reduce(partial_value):
    return lax.psum(partial_value.astype(jnp.bfloat16), "ell").astype(jnp.float32)


def angle_apply(share, work, init):
    return work(init, share, 0)


def multipole_reduce(partial_value):
    return lax.psum(partial_value.astype(jnp.bfloat16), "batch").astype(jnp.float32)


def local_plain(hidden_act, weight, first_moment, second_moment, wigner, quad_weight, target):
    batch_rows = hidden_act.shape[0]
    h_local = weight.shape[1]
    l_local = weight.shape[2]
    ell_start = lax.axis_index("ell") * l_local
    multipole = (ell_start + lax.iota(jnp.int32, l_local)).astype(jnp.float32)
    lens_rate = multipole * (multipole + 1.0) / (float(L) * float(L))
    loss_weight = 1.0 + 2.0 * multipole / float(L)
    own_hidden = lax.dynamic_slice_in_dim(hidden_act, lax.axis_index("batch") * h_local, h_local, 1)
    local_terms = jnp.einsum("cj,sjl->scl", own_hidden, weight, preferred_element_type=jnp.float32)
    log_power = lax.psum(local_terms, "batch")
    power_temp = jnp.exp(log_power[0])
    power_pol = jnp.exp(log_power[2])
    cross_scale = jnp.exp(0.5 * (log_power[0] + log_power[2]))
    cross_ratio = jnp.tanh(log_power[1])
    power_cross = cross_ratio * cross_scale
    power_lens = jnp.exp(log_power[3])
    rows = jnp.stack(
        [
            power_temp,
            lens_rate * power_temp,
            power_cross,
            lens_rate * power_cross,
            power_pol,
            lens_rate * power_pol,
            power_lens,
        ]
    ).astype(jnp.bfloat16)
    angle_sums = angle_reduce(forward_terms(rows, wigner))
    lensed_corr = angle_sums[0:6:2] - angle_sums[6:7] * angle_sums[1:6:2]
    back_rows = (lensed_corr * quad_weight).astype(jnp.bfloat16)

    def project_back(total, piece, start):
        return jnp.stack(
            [
                jnp.einsum(
                    "ca,la->cl", piece[table], wigner[table], preferred_element_type=jnp.float32
                )
                for table in range(3)
            ]
        )

    back_empty = jnp.zeros((3, batch_rows, l_local), jnp.float32)
    lensed_power = multipole_reduce(angle_apply(back_rows, project_back, back_empty))
    residual_grad = (loss_weight * (lensed_power - target.astype(jnp.float32)) / batch_rows).astype(
        jnp.bfloat16
    )
    back_partial = jnp.stack(
        [
            jnp.einsum(
                "cl,la->ca", residual_grad[table], wigner[table], preferred_element_type=jnp.float32
            )
            for table in range(3)
        ]
    )
    corr_grad = angle_reduce(back_partial) * quad_weight
    lens_sigma = angle_sums[6:7]
    sigma_grad = -jnp.sum(corr_grad * angle_sums[1:6:2], axis=0, keepdims=True)
    term_grad = jnp.concatenate(
        [
            corr_grad[0:1],
            -lens_sigma * corr_grad[0:1],
            corr_grad[1:2],
            -lens_sigma * corr_grad[1:2],
            corr_grad[2:3],
            -lens_sigma * corr_grad[2:3],
            sigma_grad,
        ],
        0,
    ).astype(jnp.bfloat16)

    def project_rows(total, piece, start):
        return backward_terms(piece, wigner)

    row_empty = jnp.zeros((7, batch_rows, l_local), jnp.float32)
    row_grad = multipole_reduce(angle_apply(term_grad, project_rows, row_empty))
    temp_coef = row_grad[0] + lens_rate * row_grad[1]
    cross_coef = row_grad[2] + lens_rate * row_grad[3]
    pol_coef = row_grad[4] + lens_rate * row_grad[5]
    log_grad = jnp.stack(
        [
            temp_coef * power_temp + 0.5 * cross_coef * power_cross,
            cross_coef * (1.0 - cross_ratio * cross_ratio) * cross_scale,
            pol_coef * power_pol + 0.5 * cross_coef * power_cross,
            row_grad[6] * power_lens,
        ]
    ).astype(jnp.bfloat16)
    weight_grad = jnp.einsum(
        "cj,scl->sjl", own_hidden, log_grad, preferred_element_type=jnp.float32
    )
    new_first = 0.9 * first_moment + 0.1 * weight_grad
    new_second = 0.999 * second_moment + 0.001 * weight_grad * weight_grad
    update = new_first / first_fix / (jnp.sqrt(new_second / second_fix) + 1e-08)
    new_weight = (weight.astype(jnp.float32) - 0.001 * update).astype(jnp.bfloat16)
    return (new_weight, new_first, new_second)


bf16 = jnp.bfloat16
SHRINK = 64
f32 = jnp.float32
ORDER = (0, 2, 1, 3)
PLAN = (
    "L0", "a0", "a3", "a2", "a1", "F0", "E0", "K0", "F3", "E3", "K3", "F2",
    "s0", "s3", "E2", "K2", "F1", "E1", "K1", "S3", "B0", "s2", "b0", "B2",
    "s1", "T0", "P0", "b2", "H3", "p0", "B1", "P2", "g3", "p2", "b1", "Q0",
    "P1", "c0", "Q2", "p1", "C0", "c2", "d0", "Q1", "C2", "W0", "c1", "w0",
    "d2", "C1", "G3", "W2", "F3", "d1", "w2", "W1", "d3", "w1", "W3", "w3", "U0",
    "U3",
)


def swap(value, axis, mask):
    count = lax.axis_size(axis)
    return lax.ppermute(value, axis, [(i, i ^ mask) for i in range(count)])


def call(kernel, out_shape, *args, waits=(), in_hbm=(), scratch=(), flops=0, moved=0):
    count = len(args)
    vmem = pl.BlockSpec(memory_space=pltpu.VMEM)
    hbm = pl.BlockSpec(memory_space=pl.ANY)

    def body(*refs):
        kernel(*refs[:count], *refs[count + len(waits) :])

    return pl.pallas_call(
        body,
        out_shape=out_shape,
        in_specs=[hbm if i in in_hbm else vmem for i in range(count)] + [hbm] * len(waits),
        out_specs=jax.tree.map(lambda _: vmem, out_shape),
        scratch_shapes=list(scratch),
        compiler_params=pltpu.CompilerParams(vmem_limit_bytes=3 << 20),
        cost_estimate=pl.CostEstimate(flops=flops // SHRINK, transcendentals=0, bytes_accessed=moved // SHRINK),
    )(*args, *waits)


def fetch_table(wigner, table, waits):
    _, rows, cols = wigner.shape
    pieces = 8
    step = rows // pieces

    def kernel(source, out, mark, sem):
        copies = [
            pltpu.make_async_copy(
                source.at[table, pl.ds(i * step, step)], out.at[pl.ds(i * step, step)], sem.at[i]
            )
            for i in range(pieces)
        ]
        for copy in copies:
            copy.start()
        mark[...] = jnp.zeros_like(mark)
        for copy in copies:
            copy.wait()

    return call(
        kernel,
        (pltpu.VMEM((rows, cols), bf16), jax.ShapeDtypeStruct((8, 128), f32)),
        wigner,
        waits=waits,
        in_hbm=(0,),
        scratch=[pltpu.SemaphoreType.DMA((pieces,))],
        moved=rows * cols * 4,
    )


def onto_angles(rows, table, rate=None):
    kinds = 1 if rate is None else 2
    count = rows.shape[0] // 4
    total_rows = kinds * rows.shape[0]
    depth, cols = table.shape
    step = cols // 4

    def kernel(*refs):
        if rate is None:
            lhs, tab, keep, send = refs
        else:
            row, rate_ref, tab, keep, send, lhs = refs
            for place in range(4):
                value = row[place * count : (place + 1) * count, :]
                lhs[2 * place * count : (2 * place + 1) * count, :] = value
                lhs[(2 * place + 1) * count : (2 * place + 2) * count, :] = (
                    value.astype(f32) * rate_ref[...]
                ).astype(bf16)
        for i in range(4):
            cut = slice(i * step, (i + 1) * step)
            total = jnp.dot(lhs[...], tab[:, cut], preferred_element_type=f32)
            keep[:, cut] = total[: total_rows // 2]
            send[:, cut] = total[total_rows // 2 :].astype(bf16)

    args = [rows] + ([] if rate is None else [rate]) + [table]
    return call(
        kernel,
        (
            jax.ShapeDtypeStruct((total_rows // 2, cols), f32),
            jax.ShapeDtypeStruct((total_rows // 2, cols), bf16),
        ),
        *args,
        scratch=[] if rate is None else [pltpu.VMEM((total_rows, depth), bf16)],
        flops=2 * total_rows * depth * cols,
        moved=total_rows * cols * 6,
    )


def onto_multipoles(halves, table, sigma=None, rate=None, waits=()):
    kinds = 1 if rate is None else 2
    half = halves[0].shape[0]
    rows = 2 * half
    cols, depth = table.shape
    step = cols // 4

    def kernel(*refs):
        if rate is None:
            one, two, tab, keep, send, lhs = refs
        else:
            one, two, sigma_one, sigma_two, rate_ref, tab, keep, send, lhs = refs
        lhs[:half, :] = one[...]
        lhs[half:rows, :] = two[...]
        if rate is not None:
            lhs[rows : rows + half, :] = (-(one[...].astype(f32) * sigma_one[...].astype(f32))).astype(bf16)
            lhs[rows + half :, :] = (-(two[...].astype(f32) * sigma_two[...].astype(f32))).astype(bf16)
        for i in range(4):
            cut = slice(i * step, (i + 1) * step)
            total = lax.dot_general(
                tab[cut, :], lhs[...], (((1,), (1,)), ((), ())), preferred_element_type=f32
            ).T
            if rate is not None:
                total = total[:rows] + total[rows:] * rate_ref[:, cut]
            keep[:, cut] = total
            send[:, cut] = total.astype(bf16)

    args = list(halves) + ([] if rate is None else list(sigma) + [rate]) + [table]
    return call(
        kernel,
        (jax.ShapeDtypeStruct((rows, cols), f32), jax.ShapeDtypeStruct((rows, cols), bf16)),
        *args,
        waits=waits,
        scratch=[pltpu.VMEM((kinds * rows, depth), bf16)],
        flops=2 * kinds * rows * depth * cols,
        moved=rows * cols * 6,
    )


def spectra(hidden, weight, wanted):
    rows, depth = hidden.shape
    cols = weight.shape[2]
    count = len(wanted)

    def kernel(hid, *refs):
        wgts, keeps, sends = refs[:count], refs[count : 2 * count], refs[2 * count :]
        for wgt, keep, send in zip(wgts, keeps, sends):
            total = jnp.dot(hid[...], wgt[...], preferred_element_type=f32)
            keep[...] = total
            send[...] = total.astype(bf16)

    def part(kind):
        return pl.BlockSpec((None, depth, cols), lambda i: (kind, 0, 0))

    whole = pl.BlockSpec((rows, cols), lambda i: (0, 0))
    return pl.pallas_call(
        kernel,
        grid=(1,),
        out_shape=[jax.ShapeDtypeStruct((rows, cols), f32)] * count
        + [jax.ShapeDtypeStruct((rows, cols), bf16)] * count,
        in_specs=[pl.BlockSpec((rows, depth), lambda i: (0, 0))] + [part(k) for k in wanted],
        out_specs=[whole] * (2 * count),
        compiler_params=pltpu.CompilerParams(vmem_limit_bytes=12 << 20),
    )(hidden, *[weight] * count)


def adam(hidden, log_grad, first_kind, weight, first, second, made):
    rows, depth = hidden.shape
    kinds, _, cols = log_grad.shape
    tile = depth // 2

    def kernel(hid, grad, wgt, one, two, *refs):
        new_wgt, new_one, new_two = refs[-3:]
        slope = lax.dot_general(
            hid[...], grad[...], (((0,), (0,)), ((), ())), preferred_element_type=f32
        )
        moved = 0.9 * one[...] + 0.1 * slope
        spread = 0.999 * two[...] + 0.001 * slope * slope
        new_one[...] = moved
        new_two[...] = spread
        update = moved * (1.0 / first_fix) / (jnp.sqrt(spread * (1.0 / second_fix)) + 1e-08)
        new_wgt[...] = (wgt[...].astype(f32) - 0.001 * update).astype(bf16)

    block = pl.BlockSpec((None, tile, cols), lambda s, i: (first_kind + s, i, 0))
    made = () if made is None else made
    return pl.pallas_call(
        kernel,
        grid=(kinds, depth // tile),
        out_shape=(
            jax.ShapeDtypeStruct(weight.shape, bf16),
            jax.ShapeDtypeStruct(weight.shape, f32),
            jax.ShapeDtypeStruct(weight.shape, f32),
        ),
        in_specs=[
            pl.BlockSpec((rows, tile), lambda s, i: (0, i)),
            pl.BlockSpec((None, rows, cols), lambda s, i: (s, 0, 0)),
        ]
        + [block] * 3
        + [pl.BlockSpec(memory_space=pl.ANY)] * len(made),
        out_specs=(block, block, block),
        input_output_aliases={5 + i: i for i in range(len(made))},
        compiler_params=pltpu.CompilerParams(vmem_limit_bytes=14 << 20),
        cost_estimate=pl.CostEstimate(
            flops=2 * kinds * rows * depth * cols,
            transcendentals=0,
            bytes_accessed=20 * kinds * depth * cols,
        ),
    )(hidden, log_grad, weight, first, second, *made)


def local_fast(hidden_act, weight, first_moment, second_moment, wigner, quad_weight, target):
    count = hidden_act.shape[0] // 4
    h_local = weight.shape[1]
    l_local = weight.shape[2]
    at_ell = lax.axis_index("ell")
    at_batch = lax.axis_index("batch")
    multipole = (at_ell * l_local + lax.iota(jnp.int32, l_local)).astype(f32)[None]
    lens_rate = multipole * (multipole + 1.0) / (float(L) * float(L))
    loss_weight = (1.0 + 2.0 * multipole / float(L)) / hidden_act.shape[0]
    quad = quad_weight[None]
    starts = [jnp.bitwise_xor(at_ell, position) * count for position in ORDER]
    own_hidden = jnp.concatenate(
        [
            lax.dynamic_slice(hidden_act, (start, at_batch * h_local), (count, h_local))
            for start in starts
        ]
    )
    wigner = pltpu.with_memory_space_constraint(wigner, pltpu.HBM)
    token = [own_hidden]

    def after(value):
        value, token[0] = lax.optimization_barrier((value, token[0]))
        return value

    def done(*values):
        token[0] = values[0]
        return values if len(values) > 1 else values[0]

    held, passed = {}, {}

    def begin(name, kept, sent, axis):
        held[name] = (kept, swap(sent, axis, 1))

    def join(name, axis):
        kept, received = held[name]
        total = after(kept) + received.astype(f32)
        if axis == "batch":
            kept, sent = total, total.astype(bf16)
        else:
            rows = total.shape[0] // 2
            kept, sent = total[:rows], total[rows:].astype(bf16)
        sent, kept = done(sent, kept)
        held[name] = (kept, swap(sent, axis, 2))
        passed[name] = sent

    def total_of(name):
        kept, received = held[name]
        return after(kept) + received.astype(f32)

    def spread(name, own):
        held[name] = (own, swap(own, "ell", 2))

    def widen(name):
        own, far = held[name]
        both = done(jnp.concatenate([after(own), far]))
        held[name] = (both, swap(both, "ell", 1))

    def halves_of(name):
        both, near = held[name]
        return after(both), near

    table, log_power, power, second_sum, corr, coef, made = {}, {}, {}, {}, {}, {}, [None]

    def log_spectra(_):
        wanted = (0, 3, 2, 1)
        parts = spectra(own_hidden, weight, wanted)
        done(parts[-1])
        for i, s in enumerate(wanted):
            begin(("log", s), parts[i], parts[4 + i], "batch")

    def fetch(t):
        waits = (token[0],)
        if not table:
            waits = tuple(passed["log", s] for s in range(4))
        table[t], mark = fetch_table(wigner, t, waits)
        done(mark)

    def own_target(_):
        value = after(target)
        held["target"] = done(
            jnp.concatenate([lax.dynamic_slice_in_dim(value, start, count, 1) for start in starts], 1)
        )

    def spectrum(s):
        log_power[s] = total_of(("log", s))
        if s == 1:
            power["scale"] = jnp.exp(0.5 * (log_power[0] + log_power[2]))
            power["ratio"] = jnp.tanh(log_power[1])
            power[s] = power["ratio"] * power["scale"]
        else:
            power[s] = jnp.exp(log_power[s])
        held["rows", s] = done(power[s].astype(bf16))

    def forward(t):
        rate = None if t == 3 else lens_rate
        sent, kept = done(*onto_angles(after(held["rows", t]), table[t], rate)[::-1])
        begin(("sum", t), kept, sent, "ell")

    def sigma(_):
        power["sigma"] = done(total_of(("sum", 3)))

    def correlate(x):
        sums = total_of(("sum", x))
        second_sum[x] = sums[count:]
        value = ((sums[:count] - power["sigma"] * second_sum[x]) * quad).astype(bf16)
        spread(("back", x), done(value))

    def project(x):
        sent, kept = done(*onto_multipoles(halves_of(("back", x)), table[x])[::-1])
        begin(("power", x), kept, sent, "batch")

    def pull(x):
        lensed = total_of(("power", x))
        own = held["target"][x].astype(f32)
        residual = done((loss_weight * (lensed - own)).astype(bf16))
        sent, kept = done(*onto_angles(residual, table[x])[::-1])
        begin(("corr", x), kept, sent, "ell")

    def correct(x):
        corr[x] = total_of(("corr", x)) * quad
        spread(("term", x), done(corr[x].astype(bf16)))

    def spread_sigma(_):
        spread("sigma", done(after(power["sigma"]).astype(bf16)))

    def sigma_grad(_):
        value = -(after(corr[0]) * second_sum[0] + corr[1] * second_sum[1] + corr[2] * second_sum[2])
        spread(("term", 3), done(value.astype(bf16)))

    def backward(t):
        more = (None, None) if t == 3 else (held["sigma"], lens_rate)
        halves = halves_of(("term", t))
        waits = tuple(passed["coef", before] for before in {2: (0,), 1: (2,), 3: (1,)}.get(t, ()))
        sent, kept = done(*onto_multipoles(halves, table[t], *more, waits)[::-1])
        begin(("coef", t), kept, sent, "batch")

    def update(first_kind):
        if first_kind == 3:
            slopes = [total_of(("coef", 3)) * power[3]]
        else:
            for t in (1, 0, 2):
                coef[t] = total_of(("coef", t))
            half_cross = 0.5 * coef[1] * power[1]
            slopes = [
                coef[0] * power[0] + half_cross,
                coef[1] * (1.0 - power["ratio"] * power["ratio"]) * power["scale"],
                coef[2] * power[2] + half_cross,
            ]
        log_grad = done(jnp.stack([slope.astype(bf16) for slope in slopes]))
        made[0] = adam(own_hidden, log_grad, first_kind, weight, first_moment, second_moment, made[0])

    actions = {
        "L": log_spectra, "F": fetch, "T": own_target, "E": spectrum, "K": forward, "S": sigma,
        "B": correlate, "P": project, "Q": pull, "C": correct, "H": spread_sigma, "G": sigma_grad,
        "W": backward, "U": update,
        "a": lambda s: join(("log", s), "batch"),
        "s": lambda t: join(("sum", t), "ell"),
        "p": lambda x: join(("power", x), "batch"),
        "c": lambda x: join(("corr", x), "ell"),
        "w": lambda t: join(("coef", t), "batch"),
        "b": lambda x: widen(("back", x)),
        "d": lambda t: widen(("term", t)),
        "g": lambda _: widen("sigma"),
    }
    for step in PLAN:
        actions[step[0]](int(step[1]))
    return made[0]


def solution(mesh):
    four = mesh.shape["ell"] == 4 and mesh.shape["batch"] == 4
    return jax.shard_map(
        local_fast if four else local_plain,
        mesh=mesh,
        in_specs=(
            P("groups", None),
            P("groups", "batch", "ell"),
            P("groups", "batch", "ell"),
            P("groups", "batch", "ell"),
            P(None, "ell", "batch"),
            P("batch"),
            P("groups", None, "ell"),
        ),
        out_specs=(
            P("groups", "batch", "ell"),
            P("groups", "batch", "ell"),
            P("groups", "batch", "ell"),
        ),
        check_vma=False,
    )
```

```python
import jax
import jax.numpy as jnp
from jax import lax
from jax.experimental import pallas as pl
from jax.experimental.pallas import tpu as pltpu
from jax.sharding import PartitionSpec as P

L = 8192


first_fix = 0.9999734386
second_fix = 0.0952078528


def forward_terms(rows, wigner):
    parts = []
    for table in range(3):
        parts.append(
            jnp.einsum(
                "rcl,la->rca",
                rows[2 * table : 2 * table + 2],
                wigner[table],
                preferred_element_type=jnp.float32,
            )
        )
    parts.append(
        jnp.einsum("rcl,la->rca", rows[6:7], wigner[3], preferred_element_type=jnp.float32)
    )
    return jnp.concatenate(parts, 0)


def backward_terms(piece, tables):
    parts = []
    for table in range(3):
        parts.append(
            jnp.einsum(
                "rca,la->rcl",
                piece[2 * table : 2 * table + 2],
                tables[table],
                preferred_element_type=jnp.float32,
            )
        )
    parts.append(
        jnp.einsum("rca,la->rcl", piece[6:7], tables[3], preferred_element_type=jnp.float32)
    )
    return jnp.concatenate(parts, 0)


def angle_reduce(partial_value):
    return lax.psum(partial_value.astype(jnp.bfloat16), "ell").astype(jnp.float32)


def angle_apply(share, work, init):
    return work(init, share, 0)


def multipole_reduce(partial_value):
    return lax.psum(partial_value.astype(jnp.bfloat16), "batch").astype(jnp.float32)


def local_plain(hidden_act, weight, first_moment, second_moment, wigner, quad_weight, target):
    batch_rows = hidden_act.shape[0]
    h_local = weight.shape[1]
    l_local = weight.shape[2]
    ell_start = lax.axis_index("ell") * l_local
    multipole = (ell_start + lax.iota(jnp.int32, l_local)).astype(jnp.float32)
    lens_rate = multipole * (multipole + 1.0) / (float(L) * float(L))
    loss_weight = 1.0 + 2.0 * multipole / float(L)
    own_hidden = lax.dynamic_slice_in_dim(hidden_act, lax.axis_index("batch") * h_local, h_local, 1)
    local_terms = jnp.einsum("cj,sjl->scl", own_hidden, weight, preferred_element_type=jnp.float32)
    log_power = lax.psum(local_terms, "batch")
    power_temp = jnp.exp(log_power[0])
    power_pol = jnp.exp(log_power[2])
    cross_scale = jnp.exp(0.5 * (log_power[0] + log_power[2]))
    cross_ratio = jnp.tanh(log_power[1])
    power_cross = cross_ratio * cross_scale
    power_lens = jnp.exp(log_power[3])
    rows = jnp.stack(
        [
            power_temp,
            lens_rate * power_temp,
            power_cross,
            lens_rate * power_cross,
            power_pol,
            lens_rate * power_pol,
            power_lens,
        ]
    ).astype(jnp.bfloat16)
    angle_sums = angle_reduce(forward_terms(rows, wigner))
    lensed_corr = angle_sums[0:6:2] - angle_sums[6:7] * angle_sums[1:6:2]
    back_rows = (lensed_corr * quad_weight).astype(jnp.bfloat16)

    def project_back(total, piece, start):
        return jnp.stack(
            [
                jnp.einsum(
                    "ca,la->cl", piece[table], wigner[table], preferred_element_type=jnp.float32
                )
                for table in range(3)
            ]
        )

    back_empty = jnp.zeros((3, batch_rows, l_local), jnp.float32)
    lensed_power = multipole_reduce(angle_apply(back_rows, project_back, back_empty))
    residual_grad = (loss_weight * (lensed_power - target.astype(jnp.float32)) / batch_rows).astype(
        jnp.bfloat16
    )
    back_partial = jnp.stack(
        [
            jnp.einsum(
                "cl,la->ca", residual_grad[table], wigner[table], preferred_element_type=jnp.float32
            )
            for table in range(3)
        ]
    )
    corr_grad = angle_reduce(back_partial) * quad_weight
    lens_sigma = angle_sums[6:7]
    sigma_grad = -jnp.sum(corr_grad * angle_sums[1:6:2], axis=0, keepdims=True)
    term_grad = jnp.concatenate(
        [
            corr_grad[0:1],
            -lens_sigma * corr_grad[0:1],
            corr_grad[1:2],
            -lens_sigma * corr_grad[1:2],
            corr_grad[2:3],
            -lens_sigma * corr_grad[2:3],
            sigma_grad,
        ],
        0,
    ).astype(jnp.bfloat16)

    def project_rows(total, piece, start):
        return backward_terms(piece, wigner)

    row_empty = jnp.zeros((7, batch_rows, l_local), jnp.float32)
    row_grad = multipole_reduce(angle_apply(term_grad, project_rows, row_empty))
    temp_coef = row_grad[0] + lens_rate * row_grad[1]
    cross_coef = row_grad[2] + lens_rate * row_grad[3]
    pol_coef = row_grad[4] + lens_rate * row_grad[5]
    log_grad = jnp.stack(
        [
            temp_coef * power_temp + 0.5 * cross_coef * power_cross,
            cross_coef * (1.0 - cross_ratio * cross_ratio) * cross_scale,
            pol_coef * power_pol + 0.5 * cross_coef * power_cross,
            row_grad[6] * power_lens,
        ]
    ).astype(jnp.bfloat16)
    weight_grad = jnp.einsum(
        "cj,scl->sjl", own_hidden, log_grad, preferred_element_type=jnp.float32
    )
    new_first = 0.9 * first_moment + 0.1 * weight_grad
    new_second = 0.999 * second_moment + 0.001 * weight_grad * weight_grad
    update = new_first / first_fix / (jnp.sqrt(new_second / second_fix) + 1e-08)
    new_weight = (weight.astype(jnp.float32) - 0.001 * update).astype(jnp.bfloat16)
    return (new_weight, new_first, new_second)


bf16 = jnp.bfloat16
SHRINK = 1 << 20
f32 = jnp.float32
ORDER = (0, 2, 1, 3)
PLAN = (
    "L0", "a0", "a3", "a2", "a1", "F0", "E0", "K0", "F3", "E3", "K3", "F2",
    "s0", "s3", "E2", "K2", "F1", "E1", "K1", "S3", "B0", "s2", "b0", "B2",
    "s1", "T0", "P0", "b2", "p0", "B1", "P2", "b1", "p2", "H3", "Q0", "P1",
    "g3", "c0", "p1", "Q2", "C0", "c2", "d0", "Q1", "C2", "W0", "c1", "w0",
    "d2", "C1", "G3", "W2", "d1", "w2", "d3", "F3", "W1", "w1", "W3", "w3", "U0",
    "U3",
)


def swap(value, axis, mask):
    count = lax.axis_size(axis)
    return lax.ppermute(value, axis, [(i, i ^ mask) for i in range(count)])


def call(kernel, out_shape, *args, waits=(), in_hbm=(), scratch=(), flops=0, moved=0):
    count = len(args)
    vmem = pl.BlockSpec(memory_space=pltpu.VMEM)
    hbm = pl.BlockSpec(memory_space=pl.ANY)

    def body(*refs):
        kernel(*refs[:count], *refs[count + len(waits) :])

    return pl.pallas_call(
        body,
        out_shape=out_shape,
        in_specs=[hbm if i in in_hbm else vmem for i in range(count)] + [hbm] * len(waits),
        out_specs=jax.tree.map(lambda _: vmem, out_shape),
        scratch_shapes=list(scratch),
        compiler_params=pltpu.CompilerParams(vmem_limit_bytes=3 << 20),
        cost_estimate=pl.CostEstimate(flops=flops // SHRINK, transcendentals=0, bytes_accessed=moved // SHRINK),
    )(*args, *waits)


def fetch_table(wigner, table, waits):
    _, rows, cols = wigner.shape
    pieces = 8
    step = rows // pieces

    def kernel(source, out, mark, sem):
        copies = [
            pltpu.make_async_copy(
                source.at[table, pl.ds(i * step, step)], out.at[pl.ds(i * step, step)], sem.at[i]
            )
            for i in range(pieces)
        ]
        for copy in copies:
            copy.start()
        mark[...] = jnp.zeros_like(mark)
        for copy in copies:
            copy.wait()

    return call(
        kernel,
        (pltpu.VMEM((rows, cols), bf16), jax.ShapeDtypeStruct((8, 128), f32)),
        wigner,
        waits=waits,
        in_hbm=(0,),
        scratch=[pltpu.SemaphoreType.DMA((pieces,))],
        moved=rows * cols * 4,
    )


def onto_angles(rows, table, rate=None, waits=()):
    kinds = 1 if rate is None else 2
    count = rows.shape[0] // 4
    total_rows = kinds * rows.shape[0]
    depth, cols = table.shape
    step = cols // 4

    def kernel(*refs):
        if rate is None:
            lhs, tab, keep, send = refs
        else:
            row, rate_ref, tab, keep, send, lhs = refs
            for place in range(4):
                value = row[place * count : (place + 1) * count, :]
                lhs[2 * place * count : (2 * place + 1) * count, :] = value
                lhs[(2 * place + 1) * count : (2 * place + 2) * count, :] = (
                    value.astype(f32) * rate_ref[...]
                ).astype(bf16)
        for i in range(4):
            cut = slice(i * step, (i + 1) * step)
            total = jnp.dot(lhs[...], tab[:, cut], preferred_element_type=f32)
            keep[:, cut] = total[: total_rows // 2]
            send[:, cut] = total[total_rows // 2 :].astype(bf16)

    args = [rows] + ([] if rate is None else [rate]) + [table]
    return call(
        kernel,
        (
            jax.ShapeDtypeStruct((total_rows // 2, cols), f32),
            jax.ShapeDtypeStruct((total_rows // 2, cols), bf16),
        ),
        *args,
        waits=waits,
        scratch=[] if rate is None else [pltpu.VMEM((total_rows, depth), bf16)],
        flops=2 * total_rows * depth * cols,
        moved=total_rows * cols * 6,
    )


def onto_multipoles(halves, table, sigma=None, rate=None, waits=()):
    kinds = 1 if rate is None else 2
    half = halves[0].shape[0]
    rows = 2 * half
    cols, depth = table.shape
    step = cols // 4

    def kernel(*refs):
        if rate is None:
            one, two, tab, keep, send, lhs = refs
        else:
            one, two, sigma_one, sigma_two, rate_ref, tab, keep, send, lhs = refs
        lhs[:half, :] = one[...]
        lhs[half:rows, :] = two[...]
        if rate is not None:
            lhs[rows : rows + half, :] = (-(one[...].astype(f32) * sigma_one[...].astype(f32))).astype(bf16)
            lhs[rows + half :, :] = (-(two[...].astype(f32) * sigma_two[...].astype(f32))).astype(bf16)
        for i in range(4):
            cut = slice(i * step, (i + 1) * step)
            total = lax.dot_general(
                tab[cut, :], lhs[...], (((1,), (1,)), ((), ())), preferred_element_type=f32
            ).T
            if rate is not None:
                total = total[:rows] + total[rows:] * rate_ref[:, cut]
            keep[:, cut] = total
            send[:, cut] = total.astype(bf16)

    args = list(halves) + ([] if rate is None else list(sigma) + [rate]) + [table]
    return call(
        kernel,
        (jax.ShapeDtypeStruct((rows, cols), f32), jax.ShapeDtypeStruct((rows, cols), bf16)),
        *args,
        waits=waits,
        scratch=[pltpu.VMEM((kinds * rows, depth), bf16)],
        flops=2 * kinds * rows * depth * cols,
        moved=rows * cols * 6,
    )


def spectra(hidden, weight, wanted):
    rows, depth = hidden.shape
    cols = weight.shape[2]
    count = len(wanted)

    def kernel(hid, *refs):
        wgts, keeps, sends = refs[:count], refs[count : 2 * count], refs[2 * count :]
        for wgt, keep, send in zip(wgts, keeps, sends):
            total = jnp.dot(hid[...], wgt[...], preferred_element_type=f32)
            keep[...] = total
            send[...] = total.astype(bf16)

    def part(kind):
        return pl.BlockSpec((None, depth, cols), lambda i: (kind, 0, 0))

    whole = pl.BlockSpec((rows, cols), lambda i: (0, 0))
    return pl.pallas_call(
        kernel,
        grid=(1,),
        out_shape=[jax.ShapeDtypeStruct((rows, cols), f32)] * count
        + [jax.ShapeDtypeStruct((rows, cols), bf16)] * count,
        in_specs=[pl.BlockSpec((rows, depth), lambda i: (0, 0))] + [part(k) for k in wanted],
        out_specs=[whole] * (2 * count),
        compiler_params=pltpu.CompilerParams(vmem_limit_bytes=12 << 20),
    )(hidden, *[weight] * count)


def adam(hidden, log_grad, first_kind, weight, first, second, made):
    rows, depth = hidden.shape
    kinds, _, cols = log_grad.shape
    tile = depth // 2

    def kernel(hid, grad, wgt, one, two, *refs):
        new_wgt, new_one, new_two = refs[-3:]
        slope = lax.dot_general(
            hid[...], grad[...], (((0,), (0,)), ((), ())), preferred_element_type=f32
        )
        moved = 0.9 * one[...] + 0.1 * slope
        spread = 0.999 * two[...] + 0.001 * slope * slope
        new_one[...] = moved
        new_two[...] = spread
        update = moved * (1.0 / first_fix) / (jnp.sqrt(spread * (1.0 / second_fix)) + 1e-08)
        new_wgt[...] = (wgt[...].astype(f32) - 0.001 * update).astype(bf16)

    block = pl.BlockSpec((None, tile, cols), lambda s, i: (first_kind + s, i, 0))
    made = () if made is None else made
    return pl.pallas_call(
        kernel,
        grid=(kinds, depth // tile),
        out_shape=(
            jax.ShapeDtypeStruct(weight.shape, bf16),
            jax.ShapeDtypeStruct(weight.shape, f32),
            jax.ShapeDtypeStruct(weight.shape, f32),
        ),
        in_specs=[
            pl.BlockSpec((rows, tile), lambda s, i: (0, i)),
            pl.BlockSpec((None, rows, cols), lambda s, i: (s, 0, 0)),
        ]
        + [block] * 3
        + [pl.BlockSpec(memory_space=pl.ANY)] * len(made),
        out_specs=(block, block, block),
        input_output_aliases={5 + i: i for i in range(len(made))},
        compiler_params=pltpu.CompilerParams(vmem_limit_bytes=14 << 20),
        cost_estimate=pl.CostEstimate(
            flops=2 * kinds * rows * depth * cols,
            transcendentals=0,
            bytes_accessed=20 * kinds * depth * cols,
        ),
    )(hidden, log_grad, weight, first, second, *made)


def local_fast(hidden_act, weight, first_moment, second_moment, wigner, quad_weight, target):
    count = hidden_act.shape[0] // 4
    h_local = weight.shape[1]
    l_local = weight.shape[2]
    at_ell = lax.axis_index("ell")
    at_batch = lax.axis_index("batch")
    multipole = (at_ell * l_local + lax.iota(jnp.int32, l_local)).astype(f32)[None]
    lens_rate = multipole * (multipole + 1.0) / (float(L) * float(L))
    loss_weight = (1.0 + 2.0 * multipole / float(L)) / hidden_act.shape[0]
    quad = quad_weight[None]
    starts = [jnp.bitwise_xor(at_ell, position) * count for position in ORDER]
    own_hidden = jnp.concatenate(
        [
            lax.dynamic_slice(hidden_act, (start, at_batch * h_local), (count, h_local))
            for start in starts
        ]
    )
    wigner = pltpu.with_memory_space_constraint(wigner, pltpu.HBM)
    token = [own_hidden]

    def after(value):
        value, token[0] = lax.optimization_barrier((value, token[0]))
        return value

    def done(*values):
        token[0] = values[0]
        return values if len(values) > 1 else values[0]

    held, passed = {}, {}

    def begin(name, kept, sent, axis):
        held[name] = (kept, swap(sent, axis, 1))

    def join(name, axis):
        kept, received = held[name]
        if name == ("corr", 2):
            own, arrived = held["power", 1]
            kept, arrived = lax.optimization_barrier((kept, arrived))
            held["power", 1] = (own, arrived)
        total = after(kept) + received.astype(f32)
        if axis == "batch":
            kept, sent = total, total.astype(bf16)
        else:
            rows = total.shape[0] // 2
            kept, sent = total[:rows], total[rows:].astype(bf16)
        sent, kept = done(sent, kept)
        held[name] = (kept, swap(sent, axis, 2))
        passed[name] = sent

    def total_of(name):
        kept, received = held[name]
        return after(kept) + received.astype(f32)

    def spread(name, own):
        held[name] = (own, swap(own, "ell", 2))

    def widen(name):
        own, far = held[name]
        both = done(jnp.concatenate([after(own), far]))
        held[name] = (both, swap(both, "ell", 1))

    def halves_of(name):
        both, near = held[name]
        return after(both), near

    table, log_power, power, second_sum, corr, coef, made = {}, {}, {}, {}, {}, {}, [None]

    def log_spectra(_):
        wanted = (0, 3, 2, 1)
        parts = spectra(own_hidden, weight, wanted)
        done(parts[-1])
        for i, s in enumerate(wanted):
            begin(("log", s), parts[i], parts[4 + i], "batch")

    def fetch(t):
        waits = (token[0],)
        if not table:
            waits = tuple(passed["log", s] for s in range(4))
        if ("coef", 2) in passed:
            waits += (passed["coef", 2], held["term", 3][0])
        table[t], mark = fetch_table(wigner, t, waits)
        passed["table"] = mark
        done(mark)

    def own_target(_):
        value = after(target)
        held["target"] = done(
            jnp.concatenate([lax.dynamic_slice_in_dim(value, start, count, 1) for start in starts], 1)
        )

    def spectrum(s):
        log_power[s] = total_of(("log", s))
        if s == 1:
            power["scale"] = jnp.exp(0.5 * (log_power[0] + log_power[2]))
            power["ratio"] = jnp.tanh(log_power[1])
            power[s] = power["ratio"] * power["scale"]
        else:
            power[s] = jnp.exp(log_power[s])
        held["rows", s] = done(power[s].astype(bf16))

    def forward(t):
        rate = None if t == 3 else lens_rate
        sent, kept = done(*onto_angles(after(held["rows", t]), table[t], rate)[::-1])
        begin(("sum", t), kept, sent, "ell")

    def sigma(_):
        power["sigma"] = done(total_of(("sum", 3)))

    def correlate(x):
        sums = total_of(("sum", x))
        second_sum[x] = sums[count:]
        value = ((sums[:count] - power["sigma"] * second_sum[x]) * quad).astype(bf16)
        spread(("back", x), done(value))

    def project(x):
        waits = (passed["power", 0],) if x == 2 else ()
        halves = halves_of(("back", x))
        sent, kept = done(*onto_multipoles(halves, table[x], None, None, waits)[::-1])
        begin(("power", x), kept, sent, "batch")

    def pull(x):
        lensed = total_of(("power", x))
        own = held["target"][x].astype(f32)
        residual = done((loss_weight * (lensed - own)).astype(bf16))
        waits = (passed["power", 1],) if x == 2 else ()
        sent, kept = done(*onto_angles(residual, table[x], None, waits)[::-1])
        begin(("corr", x), kept, sent, "ell")

    def correct(x):
        corr[x] = total_of(("corr", x)) * quad
        spread(("term", x), done(corr[x].astype(bf16)))

    def spread_sigma(_):
        spread("sigma", done(after(power["sigma"]).astype(bf16)))

    def sigma_grad(_):
        value = -(after(corr[0]) * second_sum[0] + corr[1] * second_sum[1] + corr[2] * second_sum[2])
        spread(("term", 3), done(value.astype(bf16)))

    def backward(t):
        more = (None, None) if t == 3 else (held["sigma"], lens_rate)
        halves = halves_of(("term", t))
        waits = tuple(passed["coef", before] for before in {2: (0,), 1: (2,)}.get(t, ()))
        if t == 1:
            waits += held["term", 3] + (passed["table"],)
        waits += tuple(held["coef", before][1] for before in {1: (0, 2)}.get(t, ()))
        sent, kept = done(*onto_multipoles(halves, table[t], *more, waits)[::-1])
        begin(("coef", t), kept, sent, "batch")

    def update(first_kind):
        if first_kind == 3:
            slopes = [total_of(("coef", 3)) * power[3]]
        else:
            for t in (1, 0, 2):
                coef[t] = total_of(("coef", t))
            half_cross = 0.5 * coef[1] * power[1]
            slopes = [
                coef[0] * power[0] + half_cross,
                coef[1] * (1.0 - power["ratio"] * power["ratio"]) * power["scale"],
                coef[2] * power[2] + half_cross,
            ]
        log_grad = done(jnp.stack([slope.astype(bf16) for slope in slopes]))
        made[0] = adam(own_hidden, log_grad, first_kind, weight, first_moment, second_moment, made[0])

    actions = {
        "L": log_spectra, "F": fetch, "T": own_target, "E": spectrum, "K": forward, "S": sigma,
        "B": correlate, "P": project, "Q": pull, "C": correct, "H": spread_sigma, "G": sigma_grad,
        "W": backward, "U": update,
        "a": lambda s: join(("log", s), "batch"),
        "s": lambda t: join(("sum", t), "ell"),
        "p": lambda x: join(("power", x), "batch"),
        "c": lambda x: join(("corr", x), "ell"),
        "w": lambda t: join(("coef", t), "batch"),
        "b": lambda x: widen(("back", x)),
        "d": lambda t: widen(("term", t)),
        "g": lambda _: widen("sigma"),
    }
    for step in PLAN:
        actions[step[0]](int(step[1]))
    return made[0]


def solution(mesh):
    four = mesh.shape["ell"] == 4 and mesh.shape["batch"] == 4
    return jax.shard_map(
        local_fast if four else local_plain,
        mesh=mesh,
        in_specs=(
            P("groups", None),
            P("groups", "batch", "ell"),
            P("groups", "batch", "ell"),
            P("groups", "batch", "ell"),
            P(None, "ell", "batch"),
            P("batch"),
            P("groups", None, "ell"),
        ),
        out_specs=(
            P("groups", "batch", "ell"),
            P("groups", "batch", "ell"),
            P("groups", "batch", "ell"),
        ),
        check_vma=False,
    )
```

```python
import jax
import jax.numpy as jnp
from jax import lax
from jax.experimental import pallas as pl
from jax.experimental.pallas import tpu as pltpu
from jax.sharding import PartitionSpec as P

L = 8192


first_fix = 0.9999734386
second_fix = 0.0952078528


def forward_terms(rows, wigner):
    parts = []
    for table in range(3):
        parts.append(
            jnp.einsum(
                "rcl,la->rca",
                rows[2 * table : 2 * table + 2],
                wigner[table],
                preferred_element_type=jnp.float32,
            )
        )
    parts.append(
        jnp.einsum("rcl,la->rca", rows[6:7], wigner[3], preferred_element_type=jnp.float32)
    )
    return jnp.concatenate(parts, 0)


def backward_terms(piece, tables):
    parts = []
    for table in range(3):
        parts.append(
            jnp.einsum(
                "rca,la->rcl",
                piece[2 * table : 2 * table + 2],
                tables[table],
                preferred_element_type=jnp.float32,
            )
        )
    parts.append(
        jnp.einsum("rca,la->rcl", piece[6:7], tables[3], preferred_element_type=jnp.float32)
    )
    return jnp.concatenate(parts, 0)


def angle_reduce(partial_value):
    return lax.psum(partial_value.astype(jnp.bfloat16), "ell").astype(jnp.float32)


def angle_apply(share, work, init):
    return work(init, share, 0)


def multipole_reduce(partial_value):
    return lax.psum(partial_value.astype(jnp.bfloat16), "batch").astype(jnp.float32)


def local_plain(hidden_act, weight, first_moment, second_moment, wigner, quad_weight, target):
    batch_rows = hidden_act.shape[0]
    h_local = weight.shape[1]
    l_local = weight.shape[2]
    ell_start = lax.axis_index("ell") * l_local
    multipole = (ell_start + lax.iota(jnp.int32, l_local)).astype(jnp.float32)
    lens_rate = multipole * (multipole + 1.0) / (float(L) * float(L))
    loss_weight = 1.0 + 2.0 * multipole / float(L)
    own_hidden = lax.dynamic_slice_in_dim(hidden_act, lax.axis_index("batch") * h_local, h_local, 1)
    local_terms = jnp.einsum("cj,sjl->scl", own_hidden, weight, preferred_element_type=jnp.float32)
    log_power = lax.psum(local_terms, "batch")
    power_temp = jnp.exp(log_power[0])
    power_pol = jnp.exp(log_power[2])
    cross_scale = jnp.exp(0.5 * (log_power[0] + log_power[2]))
    cross_ratio = jnp.tanh(log_power[1])
    power_cross = cross_ratio * cross_scale
    power_lens = jnp.exp(log_power[3])
    rows = jnp.stack(
        [
            power_temp,
            lens_rate * power_temp,
            power_cross,
            lens_rate * power_cross,
            power_pol,
            lens_rate * power_pol,
            power_lens,
        ]
    ).astype(jnp.bfloat16)
    angle_sums = angle_reduce(forward_terms(rows, wigner))
    lensed_corr = angle_sums[0:6:2] - angle_sums[6:7] * angle_sums[1:6:2]
    back_rows = (lensed_corr * quad_weight).astype(jnp.bfloat16)

    def project_back(total, piece, start):
        return jnp.stack(
            [
                jnp.einsum(
                    "ca,la->cl", piece[table], wigner[table], preferred_element_type=jnp.float32
                )
                for table in range(3)
            ]
        )

    back_empty = jnp.zeros((3, batch_rows, l_local), jnp.float32)
    lensed_power = multipole_reduce(angle_apply(back_rows, project_back, back_empty))
    residual_grad = (loss_weight * (lensed_power - target.astype(jnp.float32)) / batch_rows).astype(
        jnp.bfloat16
    )
    back_partial = jnp.stack(
        [
            jnp.einsum(
                "cl,la->ca", residual_grad[table], wigner[table], preferred_element_type=jnp.float32
            )
            for table in range(3)
        ]
    )
    corr_grad = angle_reduce(back_partial) * quad_weight
    lens_sigma = angle_sums[6:7]
    sigma_grad = -jnp.sum(corr_grad * angle_sums[1:6:2], axis=0, keepdims=True)
    term_grad = jnp.concatenate(
        [
            corr_grad[0:1],
            -lens_sigma * corr_grad[0:1],
            corr_grad[1:2],
            -lens_sigma * corr_grad[1:2],
            corr_grad[2:3],
            -lens_sigma * corr_grad[2:3],
            sigma_grad,
        ],
        0,
    ).astype(jnp.bfloat16)

    def project_rows(total, piece, start):
        return backward_terms(piece, wigner)

    row_empty = jnp.zeros((7, batch_rows, l_local), jnp.float32)
    row_grad = multipole_reduce(angle_apply(term_grad, project_rows, row_empty))
    temp_coef = row_grad[0] + lens_rate * row_grad[1]
    cross_coef = row_grad[2] + lens_rate * row_grad[3]
    pol_coef = row_grad[4] + lens_rate * row_grad[5]
    log_grad = jnp.stack(
        [
            temp_coef * power_temp + 0.5 * cross_coef * power_cross,
            cross_coef * (1.0 - cross_ratio * cross_ratio) * cross_scale,
            pol_coef * power_pol + 0.5 * cross_coef * power_cross,
            row_grad[6] * power_lens,
        ]
    ).astype(jnp.bfloat16)
    weight_grad = jnp.einsum(
        "cj,scl->sjl", own_hidden, log_grad, preferred_element_type=jnp.float32
    )
    new_first = 0.9 * first_moment + 0.1 * weight_grad
    new_second = 0.999 * second_moment + 0.001 * weight_grad * weight_grad
    update = new_first / first_fix / (jnp.sqrt(new_second / second_fix) + 1e-08)
    new_weight = (weight.astype(jnp.float32) - 0.001 * update).astype(jnp.bfloat16)
    return (new_weight, new_first, new_second)


bf16 = jnp.bfloat16
SHRINK = 1 << 20
f32 = jnp.float32
ORDER = (0, 2, 1, 3)
PLAN = (
    "L0", "a0", "a3", "a2", "a1", "F0", "E0", "K0", "F3", "E3", "K3", "F2",
    "s0", "s3", "E2", "K2", "F1", "E1", "K1", "S3", "B0", "s2", "b0", "B2",
    "s1", "T0", "P0", "b2", "p0", "B1", "P2", "b1", "p2", "H3", "Q0", "P1",
    "g3", "c0", "p1", "Q2", "C0", "c2", "d0", "Q1", "C2", "W0", "c1", "w0",
    "d2", "C1", "G3", "W2", "d1", "w2", "d3", "F3", "W1", "w1", "W3", "w3", "U0",
    "U3",
)


def swap(value, axis, mask):
    count = lax.axis_size(axis)
    return lax.ppermute(value, axis, [(i, i ^ mask) for i in range(count)])


def call(kernel, out_shape, *args, waits=(), in_hbm=(), scratch=(), flops=0, moved=0):
    count = len(args)
    vmem = pl.BlockSpec(memory_space=pltpu.VMEM)
    hbm = pl.BlockSpec(memory_space=pl.ANY)

    def body(*refs):
        kernel(*refs[:count], *refs[count + len(waits) :])

    return pl.pallas_call(
        body,
        out_shape=out_shape,
        in_specs=[hbm if i in in_hbm else vmem for i in range(count)] + [hbm] * len(waits),
        out_specs=jax.tree.map(lambda _: vmem, out_shape),
        scratch_shapes=list(scratch),
        compiler_params=pltpu.CompilerParams(vmem_limit_bytes=3 << 20),
        cost_estimate=pl.CostEstimate(flops=flops // SHRINK, transcendentals=0, bytes_accessed=moved // SHRINK),
    )(*args, *waits)


def fetch_table(wigner, table, waits):
    _, rows, cols = wigner.shape
    pieces = 8
    step = rows // pieces

    def kernel(source, out, mark, sem):
        copies = [
            pltpu.make_async_copy(
                source.at[table, pl.ds(i * step, step)], out.at[pl.ds(i * step, step)], sem.at[i]
            )
            for i in range(pieces)
        ]
        for copy in copies:
            copy.start()
        mark[...] = jnp.zeros_like(mark)
        for copy in copies:
            copy.wait()

    return call(
        kernel,
        (pltpu.VMEM((rows, cols), bf16), jax.ShapeDtypeStruct((8, 128), f32)),
        wigner,
        waits=waits,
        in_hbm=(0,),
        scratch=[pltpu.SemaphoreType.DMA((pieces,))],
        moved=rows * cols * 4,
    )


def onto_angles(rows, table, rate=None, waits=()):
    kinds = 1 if rate is None else 2
    count = rows.shape[0] // 4
    total_rows = kinds * rows.shape[0]
    depth, cols = table.shape
    step = cols // 4

    def kernel(*refs):
        if rate is None:
            lhs, tab, keep, send = refs
        else:
            row, rate_ref, tab, keep, send, lhs = refs
            for place in range(4):
                value = row[place * count : (place + 1) * count, :]
                lhs[2 * place * count : (2 * place + 1) * count, :] = value
                lhs[(2 * place + 1) * count : (2 * place + 2) * count, :] = (
                    value.astype(f32) * rate_ref[...]
                ).astype(bf16)
        for i in range(4):
            cut = slice(i * step, (i + 1) * step)
            total = jnp.dot(lhs[...], tab[:, cut], preferred_element_type=f32)
            keep[:, cut] = total[: total_rows // 2]
            send[:, cut] = total[total_rows // 2 :].astype(bf16)

    args = [rows] + ([] if rate is None else [rate]) + [table]
    return call(
        kernel,
        (
            jax.ShapeDtypeStruct((total_rows // 2, cols), f32),
            jax.ShapeDtypeStruct((total_rows // 2, cols), bf16),
        ),
        *args,
        waits=waits,
        scratch=[] if rate is None else [pltpu.VMEM((total_rows, depth), bf16)],
        flops=2 * total_rows * depth * cols,
        moved=total_rows * cols * 6,
    )


def onto_multipoles(halves, table, sigma=None, rate=None, waits=()):
    kinds = 1 if rate is None else 2
    half = halves[0].shape[0]
    rows = 2 * half
    cols, depth = table.shape
    step = cols // 4

    def kernel(*refs):
        if rate is None:
            one, two, tab, keep, send, lhs = refs
        else:
            one, two, sigma_one, sigma_two, rate_ref, tab, keep, send, lhs = refs
        lhs[:half, :] = one[...]
        lhs[half:rows, :] = two[...]
        if rate is not None:
            lhs[rows : rows + half, :] = (-(one[...].astype(f32) * sigma_one[...].astype(f32))).astype(bf16)
            lhs[rows + half :, :] = (-(two[...].astype(f32) * sigma_two[...].astype(f32))).astype(bf16)
        for i in range(4):
            cut = slice(i * step, (i + 1) * step)
            total = lax.dot_general(
                tab[cut, :], lhs[...], (((1,), (1,)), ((), ())), preferred_element_type=f32
            ).T
            if rate is not None:
                total = total[:rows] + total[rows:] * rate_ref[:, cut]
            keep[:, cut] = total
            send[:, cut] = total.astype(bf16)

    args = list(halves) + ([] if rate is None else list(sigma) + [rate]) + [table]
    return call(
        kernel,
        (jax.ShapeDtypeStruct((rows, cols), f32), jax.ShapeDtypeStruct((rows, cols), bf16)),
        *args,
        waits=waits,
        scratch=[pltpu.VMEM((kinds * rows, depth), bf16)],
        flops=2 * kinds * rows * depth * cols,
        moved=rows * cols * 6,
    )


def spectra(hidden, weight, wanted):
    rows, depth = hidden.shape
    cols = weight.shape[2]
    count = len(wanted)

    def kernel(hid, *refs):
        wgts, keeps, sends = refs[:count], refs[count : 2 * count], refs[2 * count :]
        for wgt, keep, send in zip(wgts, keeps, sends):
            total = jnp.dot(hid[...], wgt[...], preferred_element_type=f32)
            keep[...] = total
            send[...] = total.astype(bf16)

    def part(kind):
        return pl.BlockSpec((None, depth, cols), lambda i: (kind, 0, 0))

    whole = pl.BlockSpec((rows, cols), lambda i: (0, 0))
    return pl.pallas_call(
        kernel,
        grid=(1,),
        out_shape=[jax.ShapeDtypeStruct((rows, cols), f32)] * count
        + [jax.ShapeDtypeStruct((rows, cols), bf16)] * count,
        in_specs=[pl.BlockSpec((rows, depth), lambda i: (0, 0))] + [part(k) for k in wanted],
        out_specs=[whole] * (2 * count),
        compiler_params=pltpu.CompilerParams(vmem_limit_bytes=12 << 20),
    )(hidden, *[weight] * count)


def adam(hidden, log_grad, first_kind, weight, first, second, made):
    rows, depth = hidden.shape
    kinds, _, cols = log_grad.shape
    tile = depth // 2

    def kernel(hid, grad, wgt, one, two, *refs):
        new_wgt, new_one, new_two = refs[-3:]
        slope = lax.dot_general(
            hid[...], grad[...], (((0,), (0,)), ((), ())), preferred_element_type=f32
        )
        moved = 0.9 * one[...] + 0.1 * slope
        spread = 0.999 * two[...] + 0.001 * slope * slope
        new_one[...] = moved
        new_two[...] = spread
        scaled = spread * (1.0 / second_fix)
        root = scaled * lax.rsqrt(scaled)
        update = moved * (1.0 / first_fix) / (root + 1e-08)
        new_wgt[...] = (wgt[...].astype(f32) - 0.001 * update).astype(bf16)

    block = pl.BlockSpec((None, tile, cols), lambda s, i: (first_kind + s, i, 0))
    made = () if made is None else made
    return pl.pallas_call(
        kernel,
        grid=(kinds, depth // tile),
        out_shape=(
            jax.ShapeDtypeStruct(weight.shape, bf16),
            jax.ShapeDtypeStruct(weight.shape, f32),
            jax.ShapeDtypeStruct(weight.shape, f32),
        ),
        in_specs=[
            pl.BlockSpec((rows, tile), lambda s, i: (0, i)),
            pl.BlockSpec((None, rows, cols), lambda s, i: (s, 0, 0)),
        ]
        + [block] * 3
        + [pl.BlockSpec(memory_space=pl.ANY)] * len(made),
        out_specs=(block, block, block),
        input_output_aliases={5 + i: i for i in range(len(made))},
        compiler_params=pltpu.CompilerParams(vmem_limit_bytes=14 << 20),
        cost_estimate=pl.CostEstimate(
            flops=2 * kinds * rows * depth * cols,
            transcendentals=0,
            bytes_accessed=20 * kinds * depth * cols,
        ),
    )(hidden, log_grad, weight, first, second, *made)


def local_fast(hidden_act, weight, first_moment, second_moment, wigner, quad_weight, target):
    count = hidden_act.shape[0] // 4
    h_local = weight.shape[1]
    l_local = weight.shape[2]
    at_ell = lax.axis_index("ell")
    at_batch = lax.axis_index("batch")
    multipole = (at_ell * l_local + lax.iota(jnp.int32, l_local)).astype(f32)[None]
    lens_rate = multipole * (multipole + 1.0) / (float(L) * float(L))
    loss_weight = (1.0 + 2.0 * multipole / float(L)) / hidden_act.shape[0]
    quad = quad_weight[None]
    starts = [jnp.bitwise_xor(at_ell, position) * count for position in ORDER]
    own_hidden = jnp.concatenate(
        [
            lax.dynamic_slice(hidden_act, (start, at_batch * h_local), (count, h_local))
            for start in starts
        ]
    )
    wigner = pltpu.with_memory_space_constraint(wigner, pltpu.HBM)
    token = [own_hidden]

    def after(value):
        value, token[0] = lax.optimization_barrier((value, token[0]))
        return value

    def done(*values):
        token[0] = values[0]
        return values if len(values) > 1 else values[0]

    held, passed = {}, {}

    def begin(name, kept, sent, axis):
        held[name] = (kept, swap(sent, axis, 1))

    def join(name, axis):
        kept, received = held[name]
        if name == ("corr", 2):
            own, arrived = held["power", 1]
            kept, arrived = lax.optimization_barrier((kept, arrived))
            held["power", 1] = (own, arrived)
        total = after(kept) + received.astype(f32)
        if axis == "batch":
            kept, sent = total, total.astype(bf16)
        else:
            rows = total.shape[0] // 2
            kept, sent = total[:rows], total[rows:].astype(bf16)
        sent, kept = done(sent, kept)
        held[name] = (kept, swap(sent, axis, 2))
        passed[name] = sent

    def total_of(name):
        kept, received = held[name]
        return after(kept) + received.astype(f32)

    def spread(name, own):
        held[name] = (own, swap(own, "ell", 2))

    def widen(name):
        own, far = held[name]
        both = done(jnp.concatenate([after(own), far]))
        held[name] = (both, swap(both, "ell", 1))

    def halves_of(name):
        both, near = held[name]
        return after(both), near

    table, log_power, power, second_sum, corr, coef, made = {}, {}, {}, {}, {}, {}, [None]

    def log_spectra(_):
        wanted = (0, 3, 2, 1)
        parts = spectra(own_hidden, weight, wanted)
        done(parts[-1])
        for i, s in enumerate(wanted):
            begin(("log", s), parts[i], parts[4 + i], "batch")

    def fetch(t):
        waits = (token[0],)
        if not table:
            waits = tuple(passed["log", s] for s in range(4))
        if ("coef", 2) in passed:
            waits += (passed["coef", 2], held["term", 3][0])
        table[t], mark = fetch_table(wigner, t, waits)
        passed["table"] = mark
        done(mark)

    def own_target(_):
        value = after(target)
        held["target"] = done(
            jnp.concatenate([lax.dynamic_slice_in_dim(value, start, count, 1) for start in starts], 1)
        )

    def spectrum(s):
        log_power[s] = total_of(("log", s))
        if s == 1:
            power["scale"] = jnp.exp(0.5 * (log_power[0] + log_power[2]))
            power["ratio"] = jnp.tanh(log_power[1])
            power[s] = power["ratio"] * power["scale"]
        else:
            power[s] = jnp.exp(log_power[s])
        held["rows", s] = done(power[s].astype(bf16))

    def forward(t):
        rate = None if t == 3 else lens_rate
        sent, kept = done(*onto_angles(after(held["rows", t]), table[t], rate)[::-1])
        begin(("sum", t), kept, sent, "ell")

    def sigma(_):
        power["sigma"] = done(total_of(("sum", 3)))

    def correlate(x):
        sums = total_of(("sum", x))
        second_sum[x] = sums[count:]
        value = ((sums[:count] - power["sigma"] * second_sum[x]) * quad).astype(bf16)
        spread(("back", x), done(value))

    def project(x):
        waits = (passed["power", 0],) if x == 2 else ()
        halves = halves_of(("back", x))
        sent, kept = done(*onto_multipoles(halves, table[x], None, None, waits)[::-1])
        begin(("power", x), kept, sent, "batch")

    def pull(x):
        lensed = total_of(("power", x))
        own = held["target"][x].astype(f32)
        residual = done((loss_weight * (lensed - own)).astype(bf16))
        waits = (passed["power", 1],) if x == 2 else ()
        sent, kept = done(*onto_angles(residual, table[x], None, waits)[::-1])
        begin(("corr", x), kept, sent, "ell")

    def correct(x):
        corr[x] = total_of(("corr", x)) * quad
        spread(("term", x), done(corr[x].astype(bf16)))

    def spread_sigma(_):
        spread("sigma", done(after(power["sigma"]).astype(bf16)))

    def sigma_grad(_):
        value = -(after(corr[0]) * second_sum[0] + corr[1] * second_sum[1] + corr[2] * second_sum[2])
        spread(("term", 3), done(value.astype(bf16)))

    def backward(t):
        more = (None, None) if t == 3 else (held["sigma"], lens_rate)
        halves = halves_of(("term", t))
        waits = tuple(passed["coef", before] for before in {2: (0,), 1: (2,)}.get(t, ()))
        if t == 1:
            waits += held["term", 3] + (passed["table"],)
        waits += tuple(held["coef", before][1] for before in {1: (0, 2)}.get(t, ()))
        sent, kept = done(*onto_multipoles(halves, table[t], *more, waits)[::-1])
        begin(("coef", t), kept, sent, "batch")

    def update(first_kind):
        if first_kind == 3:
            slopes = [total_of(("coef", 3)) * power[3]]
        else:
            for t in (1, 0, 2):
                coef[t] = total_of(("coef", t))
            half_cross = 0.5 * coef[1] * power[1]
            slopes = [
                coef[0] * power[0] + half_cross,
                coef[1] * (1.0 - power["ratio"] * power["ratio"]) * power["scale"],
                coef[2] * power[2] + half_cross,
            ]
        log_grad = done(jnp.stack([slope.astype(bf16) for slope in slopes]))
        made[0] = adam(own_hidden, log_grad, first_kind, weight, first_moment, second_moment, made[0])

    actions = {
        "L": log_spectra, "F": fetch, "T": own_target, "E": spectrum, "K": forward, "S": sigma,
        "B": correlate, "P": project, "Q": pull, "C": correct, "H": spread_sigma, "G": sigma_grad,
        "W": backward, "U": update,
        "a": lambda s: join(("log", s), "batch"),
        "s": lambda t: join(("sum", t), "ell"),
        "p": lambda x: join(("power", x), "batch"),
        "c": lambda x: join(("corr", x), "ell"),
        "w": lambda t: join(("coef", t), "batch"),
        "b": lambda x: widen(("back", x)),
        "d": lambda t: widen(("term", t)),
        "g": lambda _: widen("sigma"),
    }
    for step in PLAN:
        actions[step[0]](int(step[1]))
    return made[0]


def solution(mesh):
    four = mesh.shape["ell"] == 4 and mesh.shape["batch"] == 4
    return jax.shard_map(
        local_fast if four else local_plain,
        mesh=mesh,
        in_specs=(
            P("groups", None),
            P("groups", "batch", "ell"),
            P("groups", "batch", "ell"),
            P("groups", "batch", "ell"),
            P(None, "ell", "batch"),
            P("batch"),
            P("groups", None, "ell"),
        ),
        out_specs=(
            P("groups", "batch", "ell"),
            P("groups", "batch", "ell"),
            P("groups", "batch", "ell"),
        ),
        check_vma=False,
    )
```

```python
import jax
import jax.numpy as jnp
from jax import lax
from jax.experimental import pallas as pl
from jax.experimental.pallas import tpu as pltpu
from jax.sharding import PartitionSpec as P

L = 8192


first_fix = 0.9999734386
second_fix = 0.0952078528


def forward_terms(rows, wigner):
    parts = []
    for table in range(3):
        parts.append(
            jnp.einsum(
                "rcl,la->rca",
                rows[2 * table : 2 * table + 2],
                wigner[table],
                preferred_element_type=jnp.float32,
            )
        )
    parts.append(
        jnp.einsum("rcl,la->rca", rows[6:7], wigner[3], preferred_element_type=jnp.float32)
    )
    return jnp.concatenate(parts, 0)


def backward_terms(piece, tables):
    parts = []
    for table in range(3):
        parts.append(
            jnp.einsum(
                "rca,la->rcl",
                piece[2 * table : 2 * table + 2],
                tables[table],
                preferred_element_type=jnp.float32,
            )
        )
    parts.append(
        jnp.einsum("rca,la->rcl", piece[6:7], tables[3], preferred_element_type=jnp.float32)
    )
    return jnp.concatenate(parts, 0)


def angle_reduce(partial_value):
    return lax.psum(partial_value.astype(jnp.bfloat16), "ell").astype(jnp.float32)


def angle_apply(share, work, init):
    return work(init, share, 0)


def multipole_reduce(partial_value):
    return lax.psum(partial_value.astype(jnp.bfloat16), "batch").astype(jnp.float32)


def local_plain(hidden_act, weight, first_moment, second_moment, wigner, quad_weight, target):
    batch_rows = hidden_act.shape[0]
    h_local = weight.shape[1]
    l_local = weight.shape[2]
    ell_start = lax.axis_index("ell") * l_local
    multipole = (ell_start + lax.iota(jnp.int32, l_local)).astype(jnp.float32)
    lens_rate = multipole * (multipole + 1.0) / (float(L) * float(L))
    loss_weight = 1.0 + 2.0 * multipole / float(L)
    own_hidden = lax.dynamic_slice_in_dim(hidden_act, lax.axis_index("batch") * h_local, h_local, 1)
    local_terms = jnp.einsum("cj,sjl->scl", own_hidden, weight, preferred_element_type=jnp.float32)
    log_power = lax.psum(local_terms, "batch")
    power_temp = jnp.exp(log_power[0])
    power_pol = jnp.exp(log_power[2])
    cross_scale = jnp.exp(0.5 * (log_power[0] + log_power[2]))
    cross_ratio = jnp.tanh(log_power[1])
    power_cross = cross_ratio * cross_scale
    power_lens = jnp.exp(log_power[3])
    rows = jnp.stack(
        [
            power_temp,
            lens_rate * power_temp,
            power_cross,
            lens_rate * power_cross,
            power_pol,
            lens_rate * power_pol,
            power_lens,
        ]
    ).astype(jnp.bfloat16)
    angle_sums = angle_reduce(forward_terms(rows, wigner))
    lensed_corr = angle_sums[0:6:2] - angle_sums[6:7] * angle_sums[1:6:2]
    back_rows = (lensed_corr * quad_weight).astype(jnp.bfloat16)

    def project_back(total, piece, start):
        return jnp.stack(
            [
                jnp.einsum(
                    "ca,la->cl", piece[table], wigner[table], preferred_element_type=jnp.float32
                )
                for table in range(3)
            ]
        )

    back_empty = jnp.zeros((3, batch_rows, l_local), jnp.float32)
    lensed_power = multipole_reduce(angle_apply(back_rows, project_back, back_empty))
    residual_grad = (loss_weight * (lensed_power - target.astype(jnp.float32)) / batch_rows).astype(
        jnp.bfloat16
    )
    back_partial = jnp.stack(
        [
            jnp.einsum(
                "cl,la->ca", residual_grad[table], wigner[table], preferred_element_type=jnp.float32
            )
            for table in range(3)
        ]
    )
    corr_grad = angle_reduce(back_partial) * quad_weight
    lens_sigma = angle_sums[6:7]
    sigma_grad = -jnp.sum(corr_grad * angle_sums[1:6:2], axis=0, keepdims=True)
    term_grad = jnp.concatenate(
        [
            corr_grad[0:1],
            -lens_sigma * corr_grad[0:1],
            corr_grad[1:2],
            -lens_sigma * corr_grad[1:2],
            corr_grad[2:3],
            -lens_sigma * corr_grad[2:3],
            sigma_grad,
        ],
        0,
    ).astype(jnp.bfloat16)

    def project_rows(total, piece, start):
        return backward_terms(piece, wigner)

    row_empty = jnp.zeros((7, batch_rows, l_local), jnp.float32)
    row_grad = multipole_reduce(angle_apply(term_grad, project_rows, row_empty))
    temp_coef = row_grad[0] + lens_rate * row_grad[1]
    cross_coef = row_grad[2] + lens_rate * row_grad[3]
    pol_coef = row_grad[4] + lens_rate * row_grad[5]
    log_grad = jnp.stack(
        [
            temp_coef * power_temp + 0.5 * cross_coef * power_cross,
            cross_coef * (1.0 - cross_ratio * cross_ratio) * cross_scale,
            pol_coef * power_pol + 0.5 * cross_coef * power_cross,
            row_grad[6] * power_lens,
        ]
    ).astype(jnp.bfloat16)
    weight_grad = jnp.einsum(
        "cj,scl->sjl", own_hidden, log_grad, preferred_element_type=jnp.float32
    )
    new_first = 0.9 * first_moment + 0.1 * weight_grad
    new_second = 0.999 * second_moment + 0.001 * weight_grad * weight_grad
    update = new_first / first_fix / (jnp.sqrt(new_second / second_fix) + 1e-08)
    new_weight = (weight.astype(jnp.float32) - 0.001 * update).astype(jnp.bfloat16)
    return (new_weight, new_first, new_second)


bf16 = jnp.bfloat16
SHRINK = 1 << 20
f32 = jnp.float32
ORDER = (0, 2, 1, 3)
PLAN = (
    "L0", "a0", "a3", "a2", "a1", "F0", "E0", "K0", "F3", "E3", "K3", "F2",
    "s0", "s3", "E2", "K2", "F1", "E1", "K1", "S3", "B0", "s2", "b0", "B2",
    "s1", "T0", "P0", "b2", "p0", "B1", "P2", "b1", "p2", "H3", "Q0", "P1",
    "g3", "c0", "p1", "Q2", "C0", "c2", "d0", "Q1", "C2", "W0", "c1", "w0",
    "d2", "C1", "G3", "W2", "d1", "w2", "d3", "F3", "W1", "w1", "W3", "w3", "U0",
    "U3",
)


def swap(value, axis, mask):
    count = lax.axis_size(axis)
    return lax.ppermute(value, axis, [(i, i ^ mask) for i in range(count)])


def call(kernel, out_shape, *args, waits=(), in_hbm=(), scratch=(), flops=0, moved=0):
    count = len(args)
    vmem = pl.BlockSpec(memory_space=pltpu.VMEM)
    hbm = pl.BlockSpec(memory_space=pl.ANY)

    def body(*refs):
        kernel(*refs[:count], *refs[count + len(waits) :])

    return pl.pallas_call(
        body,
        out_shape=out_shape,
        in_specs=[hbm if i in in_hbm else vmem for i in range(count)] + [hbm] * len(waits),
        out_specs=jax.tree.map(lambda _: vmem, out_shape),
        scratch_shapes=list(scratch),
        compiler_params=pltpu.CompilerParams(vmem_limit_bytes=3 << 20),
        cost_estimate=pl.CostEstimate(flops=flops // SHRINK, transcendentals=0, bytes_accessed=moved // SHRINK),
    )(*args, *waits)


def fetch_table(wigner, table, waits):
    _, rows, cols = wigner.shape
    pieces = 8
    step = rows // pieces

    def kernel(source, out, mark, sem):
        copies = [
            pltpu.make_async_copy(
                source.at[table, pl.ds(i * step, step)], out.at[pl.ds(i * step, step)], sem.at[i]
            )
            for i in range(pieces)
        ]
        for copy in copies:
            copy.start()
        mark[...] = jnp.zeros_like(mark)
        for copy in copies:
            copy.wait()

    return call(
        kernel,
        (pltpu.VMEM((rows, cols), bf16), jax.ShapeDtypeStruct((8, 128), f32)),
        wigner,
        waits=waits,
        in_hbm=(0,),
        scratch=[pltpu.SemaphoreType.DMA((pieces,))],
        moved=rows * cols * 4,
    )


def onto_angles(rows, table, rate=None, waits=()):
    kinds = 1 if rate is None else 2
    count = rows.shape[0] // 4
    total_rows = kinds * rows.shape[0]
    depth, cols = table.shape
    step = cols // 4

    def kernel(*refs):
        if rate is None:
            lhs, tab, keep, send = refs
        else:
            row, rate_ref, tab, keep, send, lhs = refs
            for place in range(4):
                value = row[place * count : (place + 1) * count, :]
                lhs[2 * place * count : (2 * place + 1) * count, :] = value
                lhs[(2 * place + 1) * count : (2 * place + 2) * count, :] = (
                    value.astype(f32) * rate_ref[...]
                ).astype(bf16)
        for i in range(4):
            cut = slice(i * step, (i + 1) * step)
            total = jnp.dot(lhs[...], tab[:, cut], preferred_element_type=f32)
            keep[:, cut] = total[: total_rows // 2]
            send[:, cut] = total[total_rows // 2 :].astype(bf16)

    args = [rows] + ([] if rate is None else [rate]) + [table]
    return call(
        kernel,
        (
            jax.ShapeDtypeStruct((total_rows // 2, cols), f32),
            jax.ShapeDtypeStruct((total_rows // 2, cols), bf16),
        ),
        *args,
        waits=waits,
        scratch=[] if rate is None else [pltpu.VMEM((total_rows, depth), bf16)],
        flops=2 * total_rows * depth * cols,
        moved=total_rows * cols * 6,
    )


def onto_multipoles(halves, table, sigma=None, rate=None, waits=()):
    kinds = 1 if rate is None else 2
    half = halves[0].shape[0]
    rows = 2 * half
    cols, depth = table.shape
    step = cols // 4

    def kernel(*refs):
        if rate is None:
            one, two, tab, keep, send, lhs = refs
        else:
            one, two, sigma_one, sigma_two, rate_ref, tab, keep, send, lhs = refs
        lhs[:half, :] = one[...]
        lhs[half:rows, :] = two[...]
        if rate is not None:
            lhs[rows : rows + half, :] = (-(one[...].astype(f32) * sigma_one[...].astype(f32))).astype(bf16)
            lhs[rows + half :, :] = (-(two[...].astype(f32) * sigma_two[...].astype(f32))).astype(bf16)
        for i in range(4):
            cut = slice(i * step, (i + 1) * step)
            total = lax.dot_general(
                tab[cut, :], lhs[...], (((1,), (1,)), ((), ())), preferred_element_type=f32
            ).T
            if rate is not None:
                total = total[:rows] + total[rows:] * rate_ref[:, cut]
            keep[:, cut] = total
            send[:, cut] = total.astype(bf16)

    args = list(halves) + ([] if rate is None else list(sigma) + [rate]) + [table]
    return call(
        kernel,
        (jax.ShapeDtypeStruct((rows, cols), f32), jax.ShapeDtypeStruct((rows, cols), bf16)),
        *args,
        waits=waits,
        scratch=[pltpu.VMEM((kinds * rows, depth), bf16)],
        flops=2 * kinds * rows * depth * cols,
        moved=rows * cols * 6,
    )


def spectra(hidden, weight, wanted):
    rows, depth = hidden.shape
    cols = weight.shape[2]
    count = len(wanted)

    def kernel(hid, *refs):
        wgts, keeps, sends = refs[:count], refs[count : 2 * count], refs[2 * count :]
        for wgt, keep, send in zip(wgts, keeps, sends):
            total = jnp.dot(hid[...], wgt[...], preferred_element_type=f32)
            keep[...] = total
            send[...] = total.astype(bf16)

    def part(kind):
        return pl.BlockSpec((None, depth, cols), lambda i: (kind, 0, 0))

    whole = pl.BlockSpec((rows, cols), lambda i: (0, 0))
    return pl.pallas_call(
        kernel,
        grid=(1,),
        out_shape=[jax.ShapeDtypeStruct((rows, cols), f32)] * count
        + [jax.ShapeDtypeStruct((rows, cols), bf16)] * count,
        in_specs=[pl.BlockSpec((rows, depth), lambda i: (0, 0))] + [part(k) for k in wanted],
        out_specs=[whole] * (2 * count),
        compiler_params=pltpu.CompilerParams(vmem_limit_bytes=12 << 20),
    )(hidden, *[weight] * count)


def adam(hidden, log_grad, first_kind, weight, first, second, made):
    rows, depth = hidden.shape
    kinds, _, cols = log_grad.shape
    tile = depth // 2

    def kernel(hid, grad, wgt, one, two, *refs):
        new_wgt, new_one, new_two = refs[-3:]
        slope = lax.dot_general(
            hid[...], grad[...], (((0,), (0,)), ((), ())), preferred_element_type=f32
        )
        moved = 0.9 * one[...] + 0.1 * slope
        spread = 0.999 * two[...] + 0.001 * slope * slope
        new_one[...] = moved
        new_two[...] = spread
        scaled = spread * (1.0 / second_fix)
        root = scaled * lax.rsqrt(scaled)
        update = moved * (0.001 / first_fix) / (root + 1e-08)
        new_wgt[...] = (wgt[...].astype(f32) - update).astype(bf16)

    block = pl.BlockSpec((None, tile, cols), lambda s, i: (first_kind + s, i, 0))
    made = () if made is None else made
    return pl.pallas_call(
        kernel,
        grid=(kinds, depth // tile),
        out_shape=(
            jax.ShapeDtypeStruct(weight.shape, bf16),
            jax.ShapeDtypeStruct(weight.shape, f32),
            jax.ShapeDtypeStruct(weight.shape, f32),
        ),
        in_specs=[
            pl.BlockSpec((rows, tile), lambda s, i: (0, i)),
            pl.BlockSpec((None, rows, cols), lambda s, i: (s, 0, 0)),
        ]
        + [block] * 3
        + [pl.BlockSpec(memory_space=pl.ANY)] * len(made),
        out_specs=(block, block, block),
        input_output_aliases={5 + i: i for i in range(len(made))},
        compiler_params=pltpu.CompilerParams(vmem_limit_bytes=14 << 20),
        cost_estimate=pl.CostEstimate(
            flops=2 * kinds * rows * depth * cols,
            transcendentals=0,
            bytes_accessed=20 * kinds * depth * cols,
        ),
    )(hidden, log_grad, weight, first, second, *made)


def local_fast(hidden_act, weight, first_moment, second_moment, wigner, quad_weight, target):
    count = hidden_act.shape[0] // 4
    h_local = weight.shape[1]
    l_local = weight.shape[2]
    at_ell = lax.axis_index("ell")
    at_batch = lax.axis_index("batch")
    multipole = (at_ell * l_local + lax.iota(jnp.int32, l_local)).astype(f32)[None]
    lens_rate = multipole * (multipole + 1.0) / (float(L) * float(L))
    loss_weight = (1.0 + 2.0 * multipole / float(L)) / hidden_act.shape[0]
    quad = quad_weight[None]
    starts = [jnp.bitwise_xor(at_ell, position) * count for position in ORDER]
    own_hidden = jnp.concatenate(
        [
            lax.dynamic_slice(hidden_act, (start, at_batch * h_local), (count, h_local))
            for start in starts
        ]
    )
    wigner = pltpu.with_memory_space_constraint(wigner, pltpu.HBM)
    token = [own_hidden]

    def after(value):
        value, token[0] = lax.optimization_barrier((value, token[0]))
        return value

    def done(*values):
        token[0] = values[0]
        return values if len(values) > 1 else values[0]

    held, passed = {}, {}

    def begin(name, kept, sent, axis):
        held[name] = (kept, swap(sent, axis, 1))

    def join(name, axis):
        kept, received = held[name]
        if name == ("corr", 2):
            own, arrived = held["power", 1]
            kept, arrived = lax.optimization_barrier((kept, arrived))
            held["power", 1] = (own, arrived)
        total = after(kept) + received.astype(f32)
        if axis == "batch":
            kept, sent = total, total.astype(bf16)
        else:
            rows = total.shape[0] // 2
            kept, sent = total[:rows], total[rows:].astype(bf16)
        sent, kept = done(sent, kept)
        held[name] = (kept, swap(sent, axis, 2))
        passed[name] = sent

    def total_of(name):
        kept, received = held[name]
        return after(kept) + received.astype(f32)

    def spread(name, own):
        held[name] = (own, swap(own, "ell", 2))

    def widen(name):
        own, far = held[name]
        both = done(jnp.concatenate([after(own), far]))
        held[name] = (both, swap(both, "ell", 1))

    def halves_of(name):
        both, near = held[name]
        return after(both), near

    table, log_power, power, second_sum, corr, coef, made = {}, {}, {}, {}, {}, {}, [None]

    def log_spectra(_):
        wanted = (0, 3, 2, 1)
        parts = spectra(own_hidden, weight, wanted)
        done(parts[-1])
        for i, s in enumerate(wanted):
            begin(("log", s), parts[i], parts[4 + i], "batch")

    def fetch(t):
        waits = (token[0],)
        if not table:
            waits = tuple(passed["log", s] for s in range(4))
        if ("coef", 2) in passed:
            waits += (passed["coef", 2], held["term", 3][0])
        table[t], mark = fetch_table(wigner, t, waits)
        passed["table"] = mark
        done(mark)

    def own_target(_):
        value = after(target)
        held["target"] = done(
            jnp.concatenate([lax.dynamic_slice_in_dim(value, start, count, 1) for start in starts], 1)
        )

    def spectrum(s):
        log_power[s] = total_of(("log", s))
        if s == 1:
            power["scale"] = jnp.exp(0.5 * (log_power[0] + log_power[2]))
            power["ratio"] = jnp.tanh(log_power[1])
            power[s] = power["ratio"] * power["scale"]
        else:
            power[s] = jnp.exp(log_power[s])
        held["rows", s] = done(power[s].astype(bf16))

    def forward(t):
        rate = None if t == 3 else lens_rate
        sent, kept = done(*onto_angles(after(held["rows", t]), table[t], rate)[::-1])
        begin(("sum", t), kept, sent, "ell")

    def sigma(_):
        power["sigma"] = done(total_of(("sum", 3)))

    def correlate(x):
        sums = total_of(("sum", x))
        second_sum[x] = sums[count:]
        value = ((sums[:count] - power["sigma"] * second_sum[x]) * quad).astype(bf16)
        spread(("back", x), done(value))

    def project(x):
        waits = (passed["power", 0],) if x == 2 else ()
        halves = halves_of(("back", x))
        sent, kept = done(*onto_multipoles(halves, table[x], None, None, waits)[::-1])
        begin(("power", x), kept, sent, "batch")

    def pull(x):
        lensed = total_of(("power", x))
        own = held["target"][x].astype(f32)
        residual = done((loss_weight * (lensed - own)).astype(bf16))
        waits = (passed["power", 1],) if x == 2 else ()
        sent, kept = done(*onto_angles(residual, table[x], None, waits)[::-1])
        begin(("corr", x), kept, sent, "ell")

    def correct(x):
        corr[x] = total_of(("corr", x)) * quad
        spread(("term", x), done(corr[x].astype(bf16)))

    def spread_sigma(_):
        spread("sigma", done(after(power["sigma"]).astype(bf16)))

    def sigma_grad(_):
        value = -(after(corr[0]) * second_sum[0] + corr[1] * second_sum[1] + corr[2] * second_sum[2])
        spread(("term", 3), done(value.astype(bf16)))

    def backward(t):
        more = (None, None) if t == 3 else (held["sigma"], lens_rate)
        halves = halves_of(("term", t))
        waits = tuple(passed["coef", before] for before in {2: (0,), 1: (2,)}.get(t, ()))
        if t == 1:
            waits += held["term", 3] + (passed["table"],)
        waits += tuple(held["coef", before][1] for before in {1: (0, 2)}.get(t, ()))
        sent, kept = done(*onto_multipoles(halves, table[t], *more, waits)[::-1])
        begin(("coef", t), kept, sent, "batch")

    def update(first_kind):
        if first_kind == 3:
            slopes = [total_of(("coef", 3)) * power[3]]
        else:
            for t in (1, 0, 2):
                coef[t] = total_of(("coef", t))
            half_cross = 0.5 * coef[1] * power[1]
            slopes = [
                coef[0] * power[0] + half_cross,
                coef[1] * (1.0 - power["ratio"] * power["ratio"]) * power["scale"],
                coef[2] * power[2] + half_cross,
            ]
        log_grad = done(jnp.stack([slope.astype(bf16) for slope in slopes]))
        made[0] = adam(own_hidden, log_grad, first_kind, weight, first_moment, second_moment, made[0])

    actions = {
        "L": log_spectra, "F": fetch, "T": own_target, "E": spectrum, "K": forward, "S": sigma,
        "B": correlate, "P": project, "Q": pull, "C": correct, "H": spread_sigma, "G": sigma_grad,
        "W": backward, "U": update,
        "a": lambda s: join(("log", s), "batch"),
        "s": lambda t: join(("sum", t), "ell"),
        "p": lambda x: join(("power", x), "batch"),
        "c": lambda x: join(("corr", x), "ell"),
        "w": lambda t: join(("coef", t), "batch"),
        "b": lambda x: widen(("back", x)),
        "d": lambda t: widen(("term", t)),
        "g": lambda _: widen("sigma"),
    }
    for step in PLAN:
        actions[step[0]](int(step[1]))
    return made[0]


def solution(mesh):
    four = mesh.shape["ell"] == 4 and mesh.shape["batch"] == 4
    return jax.shard_map(
        local_fast if four else local_plain,
        mesh=mesh,
        in_specs=(
            P("groups", None),
            P("groups", "batch", "ell"),
            P("groups", "batch", "ell"),
            P("groups", "batch", "ell"),
            P(None, "ell", "batch"),
            P("batch"),
            P("groups", None, "ell"),
        ),
        out_specs=(
            P("groups", "batch", "ell"),
            P("groups", "batch", "ell"),
            P("groups", "batch", "ell"),
        ),
        check_vma=False,
    )
```
